256 devices in a mesh: chan: 16 (over z, core), ket: 4 (over y), bra: 4 (over x).
Axes of the slice: x: 4, y: 4, z: 8, core: 2. Of those that a mesh axis runs over, the one named last changes fastest.
Arguments:
- environment: bfloat16 [16, 2048, 2048], P('chan', 'bra', 'ket'), may hold values from -6 to 6
- ket_tensor: bfloat16 [4, 2048, 2048], P(None, 'chan', 'ket'), may hold values from -0.375 to 0.375
- bra_tensor: bfloat16 [4, 2048, 2048], P(None, 'bra', 'chan'), may hold values from -0.5 to 0.5
- charge_left: int32 [2048], replicated, may hold values from 0 to 5, as said below
- charge_right: int32 [2048], replicated, may hold values from 0 to 7, as said below
- op_in: int32 [128], replicated, may hold values from 0 to 15
- op_out: int32 [128], replicated, may hold values from 0 to 15
- op_bra: int32 [128], replicated, may hold values from 0 to 3
- op_ket: int32 [128], replicated, may hold values from 0 to 3
- op_code: int32 [128], replicated, may hold values from -4 to 4
Outputs:
- new_environment: float32 [16, 2048, 2048], P('chan', 'bra', 'ket')
The draws below stay inside these ranges and needn't reach their ends.
Inputs may be any that keep to these rules, and one draw needn't show every extreme that they name: `charge_left`: charges never fall along the bond, so each charge sector is one contiguous run of states; every charge from 0 to 5 has a sector of one or more states. `charge_right`: charges never fall along the bond, so each charge sector is one contiguous run of states; every charge from 0 to 7 has a sector of one or more states.
All inputs are finite; a program needn't handle non-finite values.
Results may differ from the reference program's by a relative error of at most 0.004.
Values may be sent and summed in bfloat16 or wider, within the bound.
No kernel may reach another device: no remote copies, remote signals or barrier semaphores. Data moves between devices by JAX's collectives and lax.ppermute only.
A program may use at most 64 MiB of HBM per device.

```python
import jax
import jax.numpy as jnp
from jax import lax

W = 16
M = 2048
MR = 2048
TERMS = 128


def sector_charges(key, count, profile):
    base = jnp.array(profile, dtype=jnp.int32)
    jitter = jax.random.randint(key, base.shape, 0, 8, dtype=jnp.int32)
    weights = base * 8 + jitter
    total = jnp.sum(weights)
    ends = jnp.cumsum(weights) * count // total
    position = jnp.arange(count, dtype=jnp.int32)
    return jnp.sum((position[:, None] >= ends[None, :-1]).astype(jnp.int32), axis=1).astype(jnp.int32)


def draw_charge_left(key, part):
    return sector_charges(jax.random.fold_in(key, 11), M, [1, 5, 8, 8, 5, 1])


def draw_charge_right(key, part):
    return sector_charges(jax.random.fold_in(key, 23), MR, [1, 3, 6, 8, 8, 6, 3, 1])


def plant(values, stream_key, low, largest):
    place = [jax.random.randint(jax.random.fold_in(stream_key, axis), (), 0, length) for axis, length in enumerate(values.shape)]
    longest = values.shape.index(max(values.shape))
    next_to = place[:longest] + [(place[longest] + 1) % values.shape[longest]] + place[longest + 1:]
    return values.at[tuple(place)].set(low).at[tuple(next_to)].set(largest)


def strengthened(entries, stream_key, source, target, parts, factor):
    def block_of(axis_at):
        return (jnp.arange(entries.shape[axis_at]) // (entries.shape[axis_at] // parts)).reshape((-1,) + (1,) * (entries.ndim - 1 - axis_at))

    near = jax.random.permutation(stream_key, parts)[block_of(target)]
    other_side = (block_of(target) + parts // 2) % parts
    return jnp.where((block_of(source) == near) | (block_of(source) == other_side), factor * entries, entries)


def shard_levels(rng, shape, pieces, least, largest):
    def one(dim, shards_of):
        heights = jax.random.uniform(jax.random.fold_in(jax.random.fold_in(rng, 6), dim), (shards_of,), jnp.float32, least / len(pieces), largest / len(pieces))
        return jnp.repeat(jnp.exp(heights), shape[dim] // shards_of).reshape((-1,) + (1,) * (len(shape) - dim - 1))

    gain = one(*pieces[0])
    for cut in pieces[1:]:
        gain = gain * one(*cut)
    return gain


def centred(key, dims, deviation, reach, split=(), held_as=jnp.bfloat16):
    loudness = shard_levels(key, dims, split, -0.22, 0.18) if split else 1.0
    values = jax.random.normal(key, dims, jnp.float32) * deviation * loudness
    return jnp.minimum(jnp.maximum(values, -reach), reach).astype(held_as)


def heavy_noise(own_key, extent, spread, bound, split, heavy, kind=jnp.bfloat16):
    values = spread * jax.random.normal(own_key, extent, jnp.float32)
    if split:
        values = values * shard_levels(own_key, extent, split, -0.22, 0.18)
    return jnp.clip(strengthened(values, jax.random.fold_in(own_key, 3), *heavy), -bound, bound).astype(kind)


def setup_inputs(seed: int = 0) -> dict:
    arg_keys = jax.random.split(jax.random.key(seed), 11)
    environment = centred(arg_keys[0], (W, M, M), 1.0, 6.0, ((0, 16), (1, 4), (2, 4)))
    ket_tensor = centred(arg_keys[1], (4, M, MR), (M // 8) ** -0.5, 0.375, ((1, 16), (2, 4)))
    bra_tensor = heavy_noise(arg_keys[2], (4, M, MR), (M // 8) ** -0.5, 0.5, ((1, 4), (2, 16)), (1, 2, 16, 2.0))
    charge_left = draw_charge_left(jax.random.fold_in(arg_keys[10], 71), 0)
    charge_right = draw_charge_right(jax.random.fold_in(arg_keys[10], 71), 0)
    op_in = plant(jax.random.randint(arg_keys[5], (TERMS,), 0, W), jax.random.fold_in(arg_keys[5], 1), 0, W - 1).astype(jnp.int32)
    op_out = plant(jax.random.randint(arg_keys[6], (TERMS,), 0, W), jax.random.fold_in(arg_keys[6], 1), 0, W - 1).astype(jnp.int32)
    op_bra = plant(jax.random.randint(arg_keys[7], (TERMS,), 0, 4), jax.random.fold_in(arg_keys[7], 1), 0, 3).astype(jnp.int32)
    op_ket = plant(jax.random.randint(arg_keys[8], (TERMS,), 0, 4), jax.random.fold_in(arg_keys[8], 1), 0, 3).astype(jnp.int32)
    op_code = plant(jax.random.randint(arg_keys[9], (TERMS,), -4, 5), jax.random.fold_in(arg_keys[9], 1), -4, 4).astype(jnp.int32)
    return dict(environment=environment, ket_tensor=ket_tensor, bra_tensor=bra_tensor, charge_left=charge_left, charge_right=charge_right, op_in=op_in, op_out=op_out, op_bra=op_bra, op_ket=op_ket, op_code=op_code)


def build_coupling(op_in, op_out, op_bra, op_ket, op_code):
    slots = jnp.arange(4 * W, dtype=jnp.int32)
    pick_in = (((op_in * 4 + op_ket)[:, None]) == slots[None, :]).astype(jnp.float32)
    pick_out = (((op_out * 4 + op_bra)[:, None]) == slots[None, :]).astype(jnp.float32)
    weights = op_code.astype(jnp.float32) * 0.25
    table = jnp.dot(pick_in.T, pick_out * weights[:, None], precision=lax.Precision.HIGHEST)
    return table.reshape(W, 4, W, 4)


def reference(environment, ket_tensor, bra_tensor, charge_left, charge_right, op_in, op_out, op_bra, op_ket, op_code):
    phys = jnp.array([0, 1, 1, 2], dtype=jnp.int32)
    allowed = (charge_left[None, :, None] + phys[:, None, None]) == charge_right[None, None, :]
    ket_masked = jnp.where(allowed, ket_tensor, jnp.zeros((), jnp.bfloat16))
    bra_masked = jnp.where(allowed, bra_tensor, jnp.zeros((), jnp.bfloat16))
    coupling = build_coupling(op_in, op_out, op_bra, op_ket, op_code)
    env_wide = environment.astype(jnp.float32)
    bra_wide = bra_masked.astype(jnp.float32)
    block = 256
    starts = jnp.arange(MR // block, dtype=jnp.int32) * block

    def one_block(start):
        ket_block = lax.dynamic_slice_in_dim(ket_masked, start, block, 2).astype(jnp.float32)
        partial_value = jnp.einsum('wbk,skq->wsbq', env_wide, ket_block, precision=lax.Precision.HIGHEST)
        partial_value = partial_value.astype(jnp.bfloat16).astype(jnp.float32)
        mixed = jnp.einsum('wsbq,wsvt->vtbq', partial_value, coupling, precision=lax.Precision.HIGHEST)
        mixed = mixed.astype(jnp.bfloat16).astype(jnp.float32)
        return jnp.einsum('tbp,vtbq->vpq', bra_wide, mixed, precision=lax.Precision.HIGHEST)

    blocks = lax.map(one_block, starts)
    return jnp.transpose(blocks, (1, 2, 0, 3)).reshape(W, MR, MR)
```

```python
import functools

import jax
import jax.numpy as jnp
from jax import lax
from jax.experimental import pallas as pl
from jax.experimental.pallas import tpu as pltpu
from jax.sharding import PartitionSpec as P

BF16 = jnp.bfloat16
PHYS = (0, 1, 1, 2)
PLANE = (0, 0, 1, 0)
CHUNKS = ((0, 256), (256, 256))


def two_planes(x, diff):
    first = jnp.where(diff == 0, x[0], jnp.where(diff == 1, x[1], x[3]))
    return jnp.stack([first, x[2]])


def spread_coupling(op_in, op_out, op_bra, op_ket, op_code):
    rows = jnp.arange(1024, dtype=jnp.int32)
    pick_out = (rows[:, None] // 16 == (op_out * 4 + op_bra)[None, :]).astype(BF16)
    weights = op_code.astype(jnp.float32) * 0.25
    hit = (op_ket * 16 + op_in)[:, None] == rows[None, :] // 16
    pick_in = jnp.where(hit, weights[:, None], 0.0).astype(BF16)
    table = jnp.dot(pick_out, pick_in, preferred_element_type=jnp.float32)
    same = rows[:, None] % 16 == rows[None, :] % 16
    return jnp.where(same, table, 0.0).astype(BF16)


def first_kernel(yb, e0, e1, e2, e3a, e3b, ket, left, right, spread, out, env, masked, parts):
    quarter = e0.shape[1]
    half = e3a.shape[0]
    env[:, 0:quarter] = e0[...]
    env[:, quarter : 2 * quarter] = e1[...]
    env[:, 2 * quarter : 3 * quarter] = e2[...]
    env[0:half, 3 * quarter :] = e3a[...]
    env[half:, 3 * quarter :] = e3b[...]
    cols = right[...]
    for s in range(4):
        for i in range(4):
            block = yb[i] * 4
            for r in range(4):
                rows = left[pl.ds(pl.multiple_of((block + r) * 128, 128), 128), :]
                values = ket[block + r, PLANE[s]]
                allowed = rows + PHYS[s] == cols
                at = i * quarter + r * 128
                masked[at : at + 128, :] = jnp.where(allowed, values, jnp.zeros_like(values))
        product = jnp.dot(env[...], masked[...], preferred_element_type=jnp.float32)
        product = product.astype(BF16).reshape(16, 2, 16, product.shape[1])
        for h in range(2):
            parts[h, s * 256 : (s + 1) * 256, :] = product[:, h].reshape(256, -1)
    for h in range(2):
        mixed = jnp.dot(spread[...], parts[h], preferred_element_type=jnp.float32)
        out[:, h * 64 : (h + 1) * 64, :] = mixed.astype(BF16).reshape(16, 64, -1)


def second_kernel(got, bra, left, right, out, mixed, masked):
    for j in range(16):
        for h in range(2):
            for t in range(4):
                at = t * 512 + j * 32 + h * 16
                mixed[at : at + 16, :] = got[j, h * 64 + t * 16 : h * 64 + (t + 1) * 16, :]
    cols = left[...]

    def step(g, carry):
        for r in range(4):
            rows = right[pl.ds(pl.multiple_of((g * 4 + r) * 128, 128), 128), :]
            for t in range(4):
                values = bra[g * 4 + r, PLANE[t]]
                allowed = cols + PHYS[t] == rows
                masked[r * 128 : (r + 1) * 128, t * 512 : (t + 1) * 512] = jnp.where(
                    allowed, values, jnp.zeros_like(values)
                )
        total = jnp.dot(masked[...], mixed[...], preferred_element_type=jnp.float32)
        out[pl.ds(pl.multiple_of(g * 512, 512), 512), :] = total.astype(BF16)
        return carry

    lax.fori_loop(0, 4, step, 0)


def whole(shape):
    return pl.BlockSpec(shape, lambda i: (0,) * len(shape))


def first_stage(yb, pieces, ket, left, right, spread, start, width):
    column = start // width
    return pl.pallas_call(
        first_kernel,
        grid=(1,),
        out_shape=jax.ShapeDtypeStruct((16, 128, width), BF16),
        in_specs=[pl.BlockSpec(memory_space=pltpu.SMEM)]
        + [whole(p.shape) for p in pieces]
        + [
            pl.BlockSpec((16, 2, 128, width), lambda i: (0, 0, 0, column)),
            whole(left.shape),
            pl.BlockSpec((1, width), lambda i: (0, column)),
            whole(spread.shape),
        ],
        out_specs=whole((16, 128, width)),
        scratch_shapes=[
            pltpu.VMEM((512, 2048), BF16),
            pltpu.VMEM((2048, width), BF16),
            pltpu.VMEM((2, 1024, width), BF16),
        ],
        cost_estimate=pl.CostEstimate(
            flops=2 * 512 * 2048 * 4 * width, bytes_accessed=8 << 20, transcendentals=0
        ),
        name="first_stage",
    )(yb, *pieces, ket, left, right, spread)


def second_stage(got, bra, left, right):
    width = got.shape[2]
    return pl.pallas_call(
        second_kernel,
        grid=(1,),
        out_shape=jax.ShapeDtypeStruct((2048, width), BF16),
        in_specs=[whole(got.shape), whole(bra.shape), whole(left.shape), whole(right.shape)],
        out_specs=whole((2048, width)),
        scratch_shapes=[pltpu.VMEM((2048, width), BF16), pltpu.VMEM((512, 2048), BF16)],
        cost_estimate=pl.CostEstimate(
            flops=2 * 2048 * 2048 * width, bytes_accessed=7 << 20, transcendentals=0
        ),
        name="second_stage",
    )(got, bra, left, right)


def local(
    environment,
    ket_tensor,
    bra_tensor,
    charge_left,
    charge_right,
    op_in,
    op_out,
    op_bra,
    op_ket,
    op_code,
):
    chan, ket, bra = lax.axis_index("chan"), lax.axis_index("ket"), lax.axis_index("bra")
    right_cols = lax.dynamic_slice_in_dim(charge_right, ket * 512, 512)
    left_rows = lax.dynamic_slice_in_dim(charge_left, chan * 128, 128)
    ket_planes = two_planes(ket_tensor, right_cols[None, :] - left_rows[:, None])
    ket_all = lax.all_gather(ket_planes, "chan", axis=0)

    env = lax.all_to_all(environment.reshape(16, 32, 512), "chan", 0, 0, tiled=True)
    env = env.reshape(512, 512)
    up = [(i, (i + 1) % 4) for i in range(4)]
    down = [(i, (i + 3) % 4) for i in range(4)]
    env_below = lax.ppermute(env, "ket", up)
    env_above = lax.ppermute(env, "ket", down)
    far_a = lax.ppermute(env_below[:256], "ket", up)
    far_b = lax.ppermute(env_above[256:], "ket", down)
    yb = (ket + jnp.array([0, 3, 1, 2], jnp.int32)) % 4

    left_bra = lax.dynamic_slice_in_dim(charge_left, bra * 512, 512)
    right_bra = lax.dynamic_slice_in_dim(charge_right, chan * 128, 128)
    bra_planes = two_planes(bra_tensor, right_bra[None, :] - left_bra[:, None])
    bra_all = lax.all_gather(jnp.swapaxes(bra_planes, 1, 2), "chan", axis=0)

    spread = spread_coupling(op_in, op_out, op_bra, op_ket, op_code)
    left_column = charge_left.astype(BF16)[:, None]
    right_column = charge_right.astype(BF16)[:, None]
    left_row = left_bra.astype(BF16)[None, :]
    right_row = right_cols.astype(BF16)[None, :]

    pieces = (env, env_below, env_above, far_a, far_b)
    outs = []
    for start, width in CHUNKS:
        mixed = first_stage(yb, pieces, ket_all, left_column, right_row, spread, start, width)
        got = lax.all_to_all(mixed, "chan", 0, 0, tiled=True)
        terms = second_stage(got, bra_all, left_row, right_column)
        outs.append(lax.psum_scatter(terms, "bra", scatter_dimension=0, tiled=True))
    return jnp.concatenate(outs, axis=1).astype(jnp.float32)[None]


def solution(mesh):
    placed = (
        P("chan", "bra", "ket"),
        P(None, "chan", "ket"),
        P(None, "bra", "chan"),
        P(),
        P(),
        P(),
        P(),
        P(),
        P(),
        P(),
    )
    return jax.shard_map(
        local, mesh=mesh, in_specs=placed, out_specs=P("chan", "bra", "ket"), check_vma=False
    )
```

```python
import functools

import jax
import jax.numpy as jnp
from jax import lax
from jax.experimental import pallas as pl
from jax.experimental.pallas import tpu as pltpu
from jax.sharding import PartitionSpec as P

BF16 = jnp.bfloat16
F32 = jnp.float32
PHYS = (0, 1, 1, 2)
PLANE = (0, 0, 1, 0)
WIDTH = 256


def spread_coupling(op_in, op_out, op_bra, op_ket, op_code):
    rows = jnp.arange(1024, dtype=jnp.int32)
    pick_out = (rows[:, None] // 16 == (op_out * 4 + op_bra)[None, :]).astype(BF16)
    weights = op_code.astype(F32) * 0.25
    hit = (op_ket * 16 + op_in)[:, None] == rows[None, :] // 16
    pick_in = jnp.where(hit, weights[:, None], 0.0).astype(BF16)
    table = jnp.dot(pick_out, pick_in, preferred_element_type=F32)
    same = rows[:, None] % 16 == rows[None, :] % 16
    return jnp.where(same, table, 0.0).astype(BF16)


def charge_row(charges, block):
    return charges[pl.ds(block, 1), :].astype(F32)


def charge_column(charges, block):
    return jnp.transpose(jnp.broadcast_to(charge_row(charges, block), (128, 128)))


def chosen(x, diff):
    diff = diff.astype(BF16)
    return jnp.where(diff == 0, x[0], jnp.where(diff == 1, x[1], x[3]))


def pack_kernel(ket, bra, left, right, out):
    chan, y, x = lax.axis_index("chan"), lax.axis_index("ket"), lax.axis_index("bra")
    rows = charge_column(left, chan)
    for r in range(4):
        cut = slice(r * 128, (r + 1) * 128)
        diff = charge_row(right, y * 4 + r) - rows
        out[0, :, cut] = chosen([ket[s, :, cut] for s in range(4)], diff)
    out[1] = ket[2]
    cols = charge_row(right, chan)
    for r in range(4):
        cut = slice(r * 128, (r + 1) * 128)
        diff = cols - charge_column(left, x * 4 + r)
        first = chosen([bra[t, cut, :] for t in range(4)], diff)
        out[2, :, cut] = jnp.transpose(first.astype(F32)).astype(BF16)
        out[3, :, cut] = jnp.transpose(bra[2, cut, :].astype(F32)).astype(BF16)


def masked_tiles(values, rows, cols, charge):
    tiles = []
    for r, col in enumerate(cols):
        part = values[:, r * 128 : (r + 1) * 128]
        tiles.append(jnp.where(rows + charge == col, part, jnp.zeros_like(part)))
    return jnp.concatenate(tiles, axis=1)


def first_kernel(
    start, left_s, right_s, e0, e1, e2, e3a, e3b, planes, left, right, spread, out, env, column, acc, parts
):
    y = lax.axis_index("ket")
    width = acc.shape[1]
    for i, e in enumerate((e0, e1, e2)):
        block = lax.rem(y + (0, 3, 1)[i], 4)
        for h in range(2):
            env[2 * block + h] = e[:, h * 256 : (h + 1) * 256]
    block = lax.rem(y + 2, 4)
    for h in range(2):
        env[2 * block + h, 0:256] = e3a[:, h * 256 : (h + 1) * 256]
        env[2 * block + h, 256:512] = e3b[:, h * 256 : (h + 1) * 256]
    for c in range(16):
        column[c * 128 : (c + 1) * 128, :] = charge_column(left, c).astype(BF16)
    at = y * 4 + start // 128
    cols = [charge_row(right, at + r).astype(BF16) for r in range(width // 128)]
    least, most = right_s[y * 512 + start], right_s[y * 512 + start + width - 1]
    for s in range(4):
        acc[...] = jnp.zeros_like(acc)
        low = sum((left_s[256 * i + 255] + PHYS[s] < least).astype(jnp.int32) for i in range(8))
        high = sum((left_s[256 * i] + PHYS[s] <= most).astype(jnp.int32) for i in range(8))

        def step(i, carry):
            tiles = []
            for r in range(2):
                rows = column[pl.ds(pl.multiple_of(i * 256 + r * 128, 128), 128), :]
                values = planes[2 * i + r, PLANE[s]]
                tiles.append(masked_tiles(values, rows, cols, PHYS[s]))
            block = jnp.concatenate(tiles, axis=0)
            acc[...] += jnp.dot(env[i], block, preferred_element_type=F32)
            return carry

        lax.fori_loop(low, high, step, 0)
        product = acc[...].astype(BF16).reshape(16, 2, 16, width)
        for h in range(2):
            parts[h, s * 256 : (s + 1) * 256, :] = product[:, h].reshape(256, width)
    for h in range(2):
        mixed = jnp.dot(spread[...], parts[h], preferred_element_type=F32)
        out[:, h * 64 : (h + 1) * 64, :] = mixed.astype(BF16).reshape(16, 64, width)


def second_kernel(left_s, right_s, got, planes, left, right, out, mixed, column, acc):
    x = lax.axis_index("bra")
    for j in range(16):
        for h in range(2):
            for t in range(4):
                at = (j % 8) * 32 + h * 16
                mixed[t * 2 + j // 8, at : at + 16, :] = got[j, h * 64 + t * 16 : h * 64 + (t + 1) * 16, :]
    for c in range(16):
        column[c * 128 : (c + 1) * 128, :] = charge_column(right, c).astype(BF16)
    cols = [charge_row(left, x * 4 + r).astype(BF16) for r in range(4)]

    def step(g, carry):
        acc[...] = jnp.zeros_like(acc)
        least, most = right_s[g * 512], right_s[g * 512 + 511]
        for t in range(4):
            for h in range(2):
                first = left_s[x * 512 + h * 256] + PHYS[t]
                last = left_s[x * 512 + h * 256 + 255] + PHYS[t]

                @pl.when((first <= most) & (last >= least))
                def _():
                    tiles = []
                    for r in range(4):
                        rows = column[pl.ds(pl.multiple_of(g * 512 + r * 128, 128), 128), :]
                        values = planes[g * 4 + r, PLANE[t], :, h * 256 : (h + 1) * 256]
                        tiles.append(masked_tiles(values, rows, cols[2 * h : 2 * h + 2], -PHYS[t]))
                    block = jnp.concatenate(tiles, axis=0)
                    acc[...] += jnp.dot(block, mixed[t * 2 + h], preferred_element_type=F32)

        out[pl.ds(pl.multiple_of(g * 512, 512), 512), :] = acc[...].astype(BF16)
        return carry

    lax.fori_loop(0, 4, step, 0)


def whole(x):
    return pl.BlockSpec(x.shape, lambda i: (0,) * len(x.shape))


SCALARS = pl.BlockSpec(memory_space=pltpu.SMEM)


def pack(ket_tensor, bra_tensor, left, right):
    return pl.pallas_call(
        pack_kernel,
        grid=(1,),
        out_shape=jax.ShapeDtypeStruct((4, 128, 512), BF16),
        in_specs=[whole(ket_tensor), whole(bra_tensor), whole(left), whole(right)],
        out_specs=pl.BlockSpec((4, 128, 512), lambda i: (0, 0, 0)),
        name="pack",
    )(ket_tensor, bra_tensor, left, right)


def first_stage(charge_left, charge_right, pieces, gathered, left, right, spread, start):
    column = start // WIDTH
    return pl.pallas_call(
        functools.partial(first_kernel, start),
        grid=(1,),
        out_shape=jax.ShapeDtypeStruct((16, 128, WIDTH), BF16),
        in_specs=[SCALARS, SCALARS]
        + [whole(p) for p in pieces]
        + [
            pl.BlockSpec((16, 2, 128, WIDTH), lambda i: (0, 0, 0, column)),
            whole(left),
            whole(right),
            whole(spread),
        ],
        out_specs=pl.BlockSpec((16, 128, WIDTH), lambda i: (0, 0, 0)),
        scratch_shapes=[
            pltpu.VMEM((8, 512, 256), BF16),
            pltpu.VMEM((2048, 128), BF16),
            pltpu.VMEM((512, WIDTH), F32),
            pltpu.VMEM((2, 1024, WIDTH), BF16),
        ],
        cost_estimate=pl.CostEstimate(
            flops=512 * 2048 * 4 * WIDTH, bytes_accessed=8 << 20, transcendentals=0
        ),
        name="first_stage",
    )(charge_left, charge_right, *pieces, gathered, left, right, spread)


def second_stage(charge_left, charge_right, got, gathered, left, right):
    return pl.pallas_call(
        second_kernel,
        grid=(1,),
        out_shape=jax.ShapeDtypeStruct((2048, WIDTH), BF16),
        in_specs=[
            SCALARS,
            SCALARS,
            whole(got),
            pl.BlockSpec((16, 2, 128, 512), lambda i: (0, 1, 0, 0)),
            whole(left),
            whole(right),
        ],
        out_specs=pl.BlockSpec((2048, WIDTH), lambda i: (0, 0)),
        scratch_shapes=[
            pltpu.VMEM((8, 256, WIDTH), BF16),
            pltpu.VMEM((2048, 128), BF16),
            pltpu.VMEM((512, WIDTH), F32),
        ],
        cost_estimate=pl.CostEstimate(
            flops=2048 * 2048 * WIDTH, bytes_accessed=7 << 20, transcendentals=0
        ),
        name="second_stage",
    )(charge_left, charge_right, got, gathered, left, right)


def local(
    environment,
    ket_tensor,
    bra_tensor,
    charge_left,
    charge_right,
    op_in,
    op_out,
    op_bra,
    op_ket,
    op_code,
):
    left, right = charge_left.reshape(16, 128), charge_right.reshape(16, 128)
    planes = pack(ket_tensor, bra_tensor, left, right)
    gathered = lax.all_gather(planes, "chan", axis=0)

    env = lax.all_to_all(environment.reshape(16, 32, 512), "chan", 0, 0, tiled=True)
    env = env.reshape(512, 512)
    up = [(i, (i + 1) % 4) for i in range(4)]
    down = [(i, (i + 3) % 4) for i in range(4)]
    env_below = lax.ppermute(env, "ket", up)
    env_above = lax.ppermute(env, "ket", down)
    far_a = lax.ppermute(env_below[:256], "ket", up)
    far_b = lax.ppermute(env_above[256:], "ket", down)
    pieces = (env, env_below, env_above, far_a, far_b)
    spread = spread_coupling(op_in, op_out, op_bra, op_ket, op_code)

    terms = []
    for start in (0, WIDTH):
        mixed = first_stage(charge_left, charge_right, pieces, gathered, left, right, spread, start)
        got = lax.all_to_all(mixed, "chan", 0, 0, tiled=True)
        terms.append(second_stage(charge_left, charge_right, got, gathered, left, right))
    one = lax.psum_scatter(terms[0], "bra", scatter_dimension=0, tiled=True).astype(F32)
    two = lax.all_to_all(terms[1].reshape(4, 512, WIDTH), "bra", 0, 0, tiled=True)
    two = jnp.sum(two.astype(F32), axis=0)
    return jnp.concatenate([one, two], axis=1)[None]


def solution(mesh):
    placed = (
        P("chan", "bra", "ket"),
        P(None, "chan", "ket"),
        P(None, "bra", "chan"),
        P(),
        P(),
        P(),
        P(),
        P(),
        P(),
        P(),
    )
    return jax.shard_map(
        local, mesh=mesh, in_specs=placed, out_specs=P("chan", "bra", "ket"), check_vma=False
    )
```

```python
import functools

import jax
import jax.numpy as jnp
from jax import lax
from jax.experimental import pallas as pl
from jax.experimental.pallas import tpu as pltpu
from jax.sharding import PartitionSpec as P

BF16 = jnp.bfloat16
F32 = jnp.float32
PHYS = (0, 1, 1, 2)
PLANE = (0, 0, 1, 0)
WIDTH = 256


def spread_coupling(op_in, op_out, op_bra, op_ket, op_code):
    rows = jnp.arange(1024, dtype=jnp.int32)
    pick_out = (rows[:, None] // 16 == (op_out * 4 + op_bra)[None, :]).astype(BF16)
    weights = op_code.astype(F32) * 0.25
    hit = (op_ket * 16 + op_in)[:, None] == rows[None, :] // 16
    pick_in = jnp.where(hit, weights[:, None], 0.0).astype(BF16)
    table = jnp.dot(pick_out, pick_in, preferred_element_type=F32)
    same = rows[:, None] % 16 == rows[None, :] % 16
    return jnp.where(same, table, 0.0).astype(BF16)


def charge_row(charges, block):
    return charges[pl.ds(block, 1), :].astype(F32)


def charge_column(charges, block):
    return jnp.transpose(jnp.broadcast_to(charge_row(charges, block), (128, 128)))


def chosen(x, diff):
    diff = diff.astype(BF16)
    return jnp.where(diff == 0, x[0], jnp.where(diff == 1, x[1], x[3]))


def pack_kernel(ket, bra, left, right, out):
    chan, y, x = lax.axis_index("chan"), lax.axis_index("ket"), lax.axis_index("bra")
    rows = charge_column(left, chan)
    for r in range(4):
        cut = slice(r * 128, (r + 1) * 128)
        diff = charge_row(right, y * 4 + r) - rows
        out[r, 0] = chosen([ket[s, :, cut] for s in range(4)], diff)
        out[r, 1] = ket[2, :, cut]
    own = pl.ds(pl.multiple_of(y * 128, 128), 128)
    diff = charge_row(right, chan) - charge_column(left, x * 4 + y)
    first = chosen([bra[t, own, :] for t in range(4)], diff)
    out[4, 0] = jnp.transpose(first.astype(F32)).astype(BF16)
    out[4, 1] = jnp.transpose(bra[2, own, :].astype(F32)).astype(BF16)


def masked_tiles(parts, rows, cols, charge):
    tiles = []
    for part, col in zip(parts, cols):
        tiles.append(jnp.where(rows + charge == col, part, jnp.zeros_like(part)))
    return jnp.concatenate(tiles, axis=1)


def begin(copies, sems):
    made = [pltpu.make_async_copy(src, dst, sems.at[n]) for n, (src, dst) in enumerate(copies)]
    for copy in made:
        copy.start()
    return made


def first_kernel(
    start, left_s, right_s, e0, e1, e2, e3a, e3b, gathered, left, right, spread,
    out, env, planes, table, column, acc, parts, results, sems, out_sems,
):
    y = lax.axis_index("ket")
    width = acc.shape[1]
    tiles = width // 128
    blocks = [lax.rem(y + n, 4) for n in (0, 3, 1, 2)]
    copies = [(gathered.at[:, pl.ds(start // 128, tiles)], planes)]
    for h in range(2):
        cut = pl.ds(h * 256, 256)
        copies += [(e.at[:, cut], env.at[2 * blocks[i] + h]) for i, e in enumerate((e0, e1, e2))]
        copies += [
            (e.at[:, cut], env.at[2 * blocks[3] + h, pl.ds(n * 256, 256)])
            for n, e in enumerate((e3a, e3b))
        ]
    copies.append((spread, table))
    copies = begin(copies, sems)
    for c in range(16):
        column[c * 128 : (c + 1) * 128, :] = charge_column(left, c).astype(BF16)
    at = y * 4 + start // 128
    cols = [charge_row(right, at + r).astype(BF16) for r in range(tiles)]
    least, most = right_s[y * 512 + start], right_s[y * 512 + start + width - 1]
    for copy in copies[:-1]:
        copy.wait()
    for s in range(4):
        acc[...] = jnp.zeros_like(acc)
        low = sum((left_s[256 * i + 255] + PHYS[s] < least).astype(jnp.int32) for i in range(8))
        high = sum((left_s[256 * i] + PHYS[s] <= most).astype(jnp.int32) for i in range(8))

        def step(i, carry):
            pair = []
            for r in range(2):
                rows = column[pl.ds(pl.multiple_of(i * 256 + r * 128, 128), 128), :]
                values = [planes[2 * i + r, q, PLANE[s]] for q in range(tiles)]
                pair.append(masked_tiles(values, rows, cols, PHYS[s]))
            block = jnp.concatenate(pair, axis=0)
            acc[...] += jnp.dot(env[i], block, preferred_element_type=F32)
            return carry

        lax.fori_loop(low, high, step, 0)
        product = acc[...].astype(BF16).reshape(16, 2, 16, width)
        for h in range(2):
            parts[h, s * 256 : (s + 1) * 256, :] = product[:, h].reshape(256, width)
    copies[-1].wait()
    sent = []
    for h in range(2):
        mixed = jnp.dot(table[...], parts[h], preferred_element_type=F32)
        results[h] = mixed.astype(BF16).reshape(16, 64, width)
        copy = pltpu.make_async_copy(results.at[h], out.at[:, pl.ds(h * 64, 64)], out_sems.at[h])
        copy.start()
        sent.append(copy)
    for copy in sent:
        copy.wait()


def second_kernel(
    left_s, right_s, got, gathered, left, right,
    out, mixed, planes, column, acc, results, sems, plane_sems, out_sems,
):
    x = lax.axis_index("bra")
    copies = []
    for t in range(4):
        for half in range(2):
            for h in range(2):
                source = got.at[pl.ds(8 * half, 8), pl.ds(h * 64 + t * 16, 16)]
                copies.append((source, mixed.at[t * 2 + half, :, pl.ds(h * 16, 16)]))
    loads = begin([(gathered.at[:, pl.ds(0, 4)], planes.at[0])], plane_sems)
    copies = begin(copies, sems)
    for g in range(1, 4):
        copy = pltpu.make_async_copy(
            gathered.at[:, pl.ds(g * 4, 4)], planes.at[g], plane_sems.at[g]
        )
        copy.start()
        loads.append(copy)
    for c in range(16):
        column[c * 128 : (c + 1) * 128, :] = charge_column(right, c).astype(BF16)
    cols = [charge_row(left, x * 4 + r).astype(BF16) for r in range(4)]
    for copy in copies:
        copy.wait()
    sent = []
    for g in range(4):
        loads[g].wait()
        acc[...] = jnp.zeros_like(acc)
        least, most = right_s[g * 512], right_s[g * 512 + 511]
        for t in range(4):
            for h in range(2):
                first = left_s[x * 512 + h * 256] + PHYS[t]
                last = left_s[x * 512 + h * 256 + 255] + PHYS[t]

                @pl.when((first <= most) & (last >= least))
                def _():
                    stack = []
                    for r in range(4):
                        rows = column[g * 512 + r * 128 : g * 512 + (r + 1) * 128, :]
                        values = [planes[g, 2 * h + q, r, PLANE[t]] for q in range(2)]
                        stack.append(masked_tiles(values, rows, cols[2 * h : 2 * h + 2], -PHYS[t]))
                    block = jnp.concatenate(stack, axis=0)
                    other = mixed[t * 2 + h].reshape(256, acc.shape[1])
                    acc[...] += jnp.dot(block, other, preferred_element_type=F32)

        results[g] = acc[...].astype(BF16)
        copy = pltpu.make_async_copy(results.at[g], out.at[pl.ds(g * 512, 512)], out_sems.at[g])
        copy.start()
        sent.append(copy)
    for copy in sent:
        copy.wait()


SCALARS = pl.BlockSpec(memory_space=pltpu.SMEM)
FAST = pl.BlockSpec(memory_space=pltpu.VMEM)
PLACE = pl.BlockSpec(memory_space=pl.ANY)


def pack(ket_tensor, bra_tensor, left, right):
    return pl.pallas_call(
        pack_kernel,
        out_shape=jax.ShapeDtypeStruct((5, 2, 128, 128), BF16),
        in_specs=[FAST] * 4,
        out_specs=FAST,
        name="pack",
    )(ket_tensor, bra_tensor, left, right)


def first_stage(charge_left, charge_right, pieces, gathered, left, right, spread, start):
    return pl.pallas_call(
        functools.partial(first_kernel, start),
        out_shape=jax.ShapeDtypeStruct((16, 128, WIDTH), BF16),
        in_specs=[SCALARS, SCALARS] + [PLACE] * (len(pieces) + 1) + [FAST, FAST, PLACE],
        out_specs=PLACE,
        scratch_shapes=[
            pltpu.VMEM((8, 512, 256), BF16),
            pltpu.VMEM((16, WIDTH // 128, 2, 128, 128), BF16),
            pltpu.VMEM((1024, 1024), BF16),
            pltpu.VMEM((2048, 128), BF16),
            pltpu.VMEM((512, WIDTH), F32),
            pltpu.VMEM((2, 1024, WIDTH), BF16),
            pltpu.VMEM((2, 16, 64, WIDTH), BF16),
            pltpu.SemaphoreType.DMA((12,)),
            pltpu.SemaphoreType.DMA((2,)),
        ],
        cost_estimate=pl.CostEstimate(
            flops=512 * 2048 * 4 * WIDTH, bytes_accessed=8 << 20, transcendentals=0
        ),
        name="first_stage",
    )(charge_left, charge_right, *pieces, gathered, left, right, spread)


def second_stage(charge_left, charge_right, got, gathered, left, right):
    return pl.pallas_call(
        second_kernel,
        out_shape=jax.ShapeDtypeStruct((2048, WIDTH), BF16),
        in_specs=[SCALARS, SCALARS, PLACE, PLACE, FAST, FAST],
        out_specs=PLACE,
        scratch_shapes=[
            pltpu.VMEM((8, 8, 32, WIDTH), BF16),
            pltpu.VMEM((4, 4, 4, 2, 128, 128), BF16),
            pltpu.VMEM((2048, 128), BF16),
            pltpu.VMEM((512, WIDTH), F32),
            pltpu.VMEM((4, 512, WIDTH), BF16),
            pltpu.SemaphoreType.DMA((16,)),
            pltpu.SemaphoreType.DMA((4,)),
            pltpu.SemaphoreType.DMA((4,)),
        ],
        cost_estimate=pl.CostEstimate(
            flops=2048 * 2048 * WIDTH, bytes_accessed=7 << 20, transcendentals=0
        ),
        name="second_stage",
    )(charge_left, charge_right, got, gathered, left, right)


def local(
    environment,
    ket_tensor,
    bra_tensor,
    charge_left,
    charge_right,
    op_in,
    op_out,
    op_bra,
    op_ket,
    op_code,
):
    left, right = charge_left.reshape(16, 128), charge_right.reshape(16, 128)
    planes = pack(ket_tensor, bra_tensor, left, right)
    gathered = lax.all_gather(planes, "chan", axis=0)

    env = lax.all_to_all(environment.reshape(16, 32, 512), "chan", 0, 0, tiled=True)
    env = env.reshape(512, 512)
    up = [(i, (i + 1) % 4) for i in range(4)]
    down = [(i, (i + 3) % 4) for i in range(4)]
    env_below = lax.ppermute(env, "ket", up)
    env_above = lax.ppermute(env, "ket", down)
    far_a = lax.ppermute(env_below[:256], "ket", up)
    far_b = lax.ppermute(env_above[256:], "ket", down)
    spread = spread_coupling(op_in, op_out, op_bra, op_ket, op_code)
    pieces = (env, env_below, env_above, far_a, far_b)
    gathered, spread, pieces = lax.optimization_barrier((gathered, spread, pieces))
    bra_gathered = lax.all_gather(gathered[:, 4], "ket", axis=0)

    terms = []
    for start in (0, WIDTH):
        mixed = first_stage(charge_left, charge_right, pieces, gathered, left, right, spread, start)
        got = lax.all_to_all(mixed, "chan", 0, 0, tiled=True)
        terms.append(second_stage(charge_left, charge_right, got, bra_gathered, left, right))
    one = lax.psum_scatter(terms[0], "bra", scatter_dimension=0, tiled=True).astype(F32)
    two = lax.all_to_all(terms[1].reshape(4, 512, WIDTH), "bra", 0, 0, tiled=True)
    two = jnp.sum(two.astype(F32), axis=0)
    return jnp.concatenate([one, two], axis=1)[None]


def solution(mesh):
    placed = (
        P("chan", "bra", "ket"),
        P(None, "chan", "ket"),
        P(None, "bra", "chan"),
        P(),
        P(),
        P(),
        P(),
        P(),
        P(),
        P(),
    )
    return jax.shard_map(
        local, mesh=mesh, in_specs=placed, out_specs=P("chan", "bra", "ket"), check_vma=False
    )
```

```python
import functools

import jax
import jax.numpy as jnp
from jax import lax
from jax.experimental import pallas as pl
from jax.experimental.pallas import tpu as pltpu
from jax.sharding import PartitionSpec as P

BF16 = jnp.bfloat16
F32 = jnp.float32
PHYS = (0, 1, 1, 2)
PLANE = (0, 0, 1, 0)
WIDTH = 256


def spread_coupling(op_in, op_out, op_bra, op_ket, op_code):
    rows = jnp.arange(1024, dtype=jnp.int32)
    pick_out = (rows[:, None] // 16 == (op_out * 4 + op_bra)[None, :]).astype(BF16)
    weights = op_code.astype(F32) * 0.25
    hit = (op_ket * 16 + op_in)[:, None] == rows[None, :] // 16
    pick_in = jnp.where(hit, weights[:, None], 0.0).astype(BF16)
    table = jnp.dot(pick_out, pick_in, preferred_element_type=F32)
    same = rows[:, None] % 16 == rows[None, :] % 16
    return jnp.where(same, table, 0.0).astype(BF16)


def charge_row(charges, block):
    return charges[pl.ds(block, 1), :].astype(F32)


def charge_column(charges, block):
    return jnp.transpose(jnp.broadcast_to(charge_row(charges, block), (128, 128)))


def chosen(x, diff):
    diff = diff.astype(BF16)
    return jnp.where(diff == 0, x[0], jnp.where(diff == 1, x[1], x[3]))


def pack_kernel(ket, bra, left, right, out):
    chan, y, x = lax.axis_index("chan"), lax.axis_index("ket"), lax.axis_index("bra")
    rows = charge_column(left, chan)
    for r in range(4):
        cut = slice(r * 128, (r + 1) * 128)
        diff = charge_row(right, y * 4 + r) - rows
        out[r, 0] = chosen([ket[s, :, cut] for s in range(4)], diff)
        out[r, 1] = ket[2, :, cut]
    own = pl.ds(pl.multiple_of(y * 128, 128), 128)
    diff = charge_row(right, chan) - charge_column(left, x * 4 + y)
    first = chosen([bra[t, own, :] for t in range(4)], diff)
    out[4, 0] = jnp.transpose(first.astype(F32)).astype(BF16)
    out[4, 1] = jnp.transpose(bra[2, own, :].astype(F32)).astype(BF16)


def masked_tiles(parts, rows, cols, charge):
    tiles = []
    for part, col in zip(parts, cols):
        tiles.append(jnp.where(rows + charge == col, part, jnp.zeros_like(part)))
    return jnp.concatenate(tiles, axis=1)


def begin(copies, sems):
    made = [pltpu.make_async_copy(src, dst, sems.at[n]) for n, (src, dst) in enumerate(copies)]
    for copy in made:
        copy.start()
    return made


def first_kernel(
    start, left_s, right_s, e0, e1, e2, e3a, e3b, gathered, left, right, spread,
    out, bra_out, env, planes, bra_planes, column, acc, parts, results, sems, out_sems,
):
    y = lax.axis_index("ket")
    width = acc.shape[1]
    tiles = width // 128
    blocks = [lax.rem(y + n, 4) for n in (0, 3, 1, 2)]
    loads = [(gathered.at[:, pl.ds(start // 128, tiles)], planes)]
    if start == 0:
        loads.append((gathered.at[:, 4], bra_planes))
    loads = begin(loads, sems)
    for h in range(2):
        cut = slice(h * 256, (h + 1) * 256)
        for i, e in enumerate((e0, e1, e2)):
            env[2 * blocks[i] + h] = e[:, cut]
        for n, e in enumerate((e3a, e3b)):
            env[2 * blocks[3] + h, n * 256 : (n + 1) * 256] = e[:, cut]
    for c in range(16):
        column[c * 128 : (c + 1) * 128, :] = charge_column(left, c).astype(BF16)
    at = y * 4 + start // 128
    cols = [charge_row(right, at + r).astype(BF16) for r in range(tiles)]
    least, most = right_s[y * 512 + start], right_s[y * 512 + start + width - 1]
    loads[0].wait()
    for s in range(4):
        acc[...] = jnp.zeros_like(acc)
        low = sum((left_s[256 * i + 255] + PHYS[s] < least).astype(jnp.int32) for i in range(8))
        high = sum((left_s[256 * i] + PHYS[s] <= most).astype(jnp.int32) for i in range(8))

        def step(i, carry):
            pair = []
            for r in range(2):
                rows = column[pl.ds(pl.multiple_of(i * 256 + r * 128, 128), 128), :]
                values = [planes[2 * i + r, q, PLANE[s]] for q in range(tiles)]
                pair.append(masked_tiles(values, rows, cols, PHYS[s]))
            block = jnp.concatenate(pair, axis=0)
            acc[...] += jnp.dot(env[i], block, preferred_element_type=F32)
            return carry

        lax.fori_loop(low, high, step, 0)
        product = acc[...].astype(BF16).reshape(16, 2, 16, width)
        for h in range(2):
            parts[h, s * 256 : (s + 1) * 256, :] = product[:, h].reshape(256, width)
    sent = []
    if start == 0:
        loads[1].wait()
        sent = begin([(bra_planes, bra_out)], out_sems.at[pl.ds(2, 1)])
    for h in range(2):
        mixed = jnp.dot(spread[...], parts[h], preferred_element_type=F32)
        results[h] = mixed.astype(BF16).reshape(16, 64, width)
        copy = pltpu.make_async_copy(results.at[h], out.at[:, pl.ds(h * 64, 64)], out_sems.at[h])
        copy.start()
        sent.append(copy)
    for copy in sent:
        copy.wait()


def active(left_s, right_s, x, g, t, h):
    least, most = right_s[g * 512], right_s[g * 512 + 511]
    first = left_s[x * 512 + h * 256] + PHYS[t]
    last = left_s[x * 512 + h * 256 + 255] + PHYS[t]
    return (first <= most) & (last >= least)


def each_active(left_s, right_s, x, act):
    for g in range(4):
        for t in range(4):
            for h in range(2):

                @pl.when(active(left_s, right_s, x, g, t, h))
                def _():
                    act(g, t * 2 + h)


def tile_copy(source, target, sems, g, n):
    return pltpu.make_async_copy(source.at[g, n], target.at[g, n], sems.at[g * 8 + n])


def mask_kernel(
    left_s, right_s, gathered, left, right, out, planes, tiles, column, sems, out_sems
):
    x = lax.axis_index("bra")
    loads = begin([(gathered.at[:, pl.ds(g * 4, 4)], planes.at[g]) for g in range(4)], sems)
    for c in range(16):
        column[c * 128 : (c + 1) * 128, :] = charge_column(right, c).astype(BF16)
    cols = [charge_row(left, x * 4 + r).astype(BF16) for r in range(4)]
    for g in range(4):
        loads[g].wait()
        for t in range(4):
            for h in range(2):

                @pl.when(active(left_s, right_s, x, g, t, h))
                def _():
                    for r in range(4):
                        rows = column[g * 512 + r * 128 : g * 512 + (r + 1) * 128, :]
                        values = [planes[g, 2 * h + q, r, PLANE[t]] for q in range(2)]
                        tile = masked_tiles(values, rows, cols[2 * h : 2 * h + 2], -PHYS[t])
                        tiles[g, t * 2 + h, r * 128 : (r + 1) * 128, :] = tile
                    tile_copy(tiles, out, out_sems, g, t * 2 + h).start()

    each_active(
        left_s, right_s, x, lambda g, n: tile_copy(tiles, out, out_sems, g, n).wait()
    )


def second_kernel(left_s, right_s, got, masked, out, mixed, acc, tiles, sems):
    x = lax.axis_index("bra")
    each_active(
        left_s, right_s, x, lambda g, n: tile_copy(masked, tiles, sems, g, n).start()
    )
    for j in range(16):
        for h in range(2):
            for t in range(4):
                at = (j % 8) * 32 + h * 16
                mixed[t * 2 + j // 8, at : at + 16, :] = got[j, h * 64 + t * 16 : h * 64 + (t + 1) * 16, :]
    for g in range(4):
        acc[...] = jnp.zeros_like(acc)
        for t in range(4):
            for h in range(2):

                @pl.when(active(left_s, right_s, x, g, t, h))
                def _():
                    n = t * 2 + h
                    tile_copy(masked, tiles, sems, g, n).wait()
                    acc[...] += jnp.dot(tiles[g, n], mixed[n], preferred_element_type=F32)

        out[g * 512 : (g + 1) * 512, :] = acc[...].astype(BF16)


def last_kernel(one, two, out):
    out[0, :, 0:WIDTH] = one[...].astype(F32)
    total = two[0].astype(F32) + two[1].astype(F32)
    out[0, :, WIDTH : 2 * WIDTH] = total + two[2].astype(F32) + two[3].astype(F32)


SCALARS = pl.BlockSpec(memory_space=pltpu.SMEM)
FAST = pl.BlockSpec(memory_space=pltpu.VMEM)
PLACE = pl.BlockSpec(memory_space=pltpu.HBM)
PARAMS = pltpu.CompilerParams(vmem_limit_bytes=24 << 20)


def held(x):
    return pltpu.with_memory_space_constraint(x, pltpu.HBM)


def pack(ket_tensor, bra_tensor, left, right):
    return pl.pallas_call(
        pack_kernel,
        out_shape=jax.ShapeDtypeStruct((5, 2, 128, 128), BF16),
        in_specs=[FAST] * 4,
        out_specs=FAST,
        name="pack",
    )(ket_tensor, bra_tensor, left, right)


def first_stage(charge_left, charge_right, pieces, gathered, left, right, spread, start):
    bra_shape = (16, 2, 128, 128) if start == 0 else (1, 2, 128, 128)
    return pl.pallas_call(
        functools.partial(first_kernel, start),
        out_shape=[
            pltpu.HBM((16, 128, WIDTH), BF16),
            pltpu.HBM(bra_shape, BF16),
        ],
        in_specs=[SCALARS, SCALARS] + [FAST] * len(pieces) + [PLACE] + [FAST] * 3,
        out_specs=[PLACE, PLACE],
        scratch_shapes=[
            pltpu.VMEM((8, 512, 256), BF16),
            pltpu.VMEM((16, WIDTH // 128, 2, 128, 128), BF16),
            pltpu.VMEM(bra_shape, BF16),
            pltpu.VMEM((2048, 128), BF16),
            pltpu.VMEM((512, WIDTH), F32),
            pltpu.VMEM((2, 1024, WIDTH), BF16),
            pltpu.VMEM((2, 16, 64, WIDTH), BF16),
            pltpu.SemaphoreType.DMA((2,)),
            pltpu.SemaphoreType.DMA((3,)),
        ],
        compiler_params=PARAMS,
        cost_estimate=pl.CostEstimate(
            flops=512 * 2048 * 4 * WIDTH, bytes_accessed=8 << 20, transcendentals=0
        ),
        name="first_stage",
    )(charge_left, charge_right, *pieces, held(gathered), left, right, spread)


def mask_bra(charge_left, charge_right, gathered, left, right):
    return pl.pallas_call(
        mask_kernel,
        out_shape=pltpu.HBM((4, 8, 512, 256), BF16),
        in_specs=[SCALARS, SCALARS, PLACE, FAST, FAST],
        out_specs=PLACE,
        scratch_shapes=[
            pltpu.VMEM((4, 4, 4, 2, 128, 128), BF16),
            pltpu.VMEM((4, 8, 512, 256), BF16),
            pltpu.VMEM((2048, 128), BF16),
            pltpu.SemaphoreType.DMA((4,)),
            pltpu.SemaphoreType.DMA((32,)),
        ],
        compiler_params=PARAMS,
        name="mask_bra",
    )(charge_left, charge_right, held(gathered), left, right)


def second_stage(charge_left, charge_right, got, masked):
    return pl.pallas_call(
        second_kernel,
        out_shape=jax.ShapeDtypeStruct((2048, WIDTH), BF16),
        in_specs=[SCALARS, SCALARS, FAST, PLACE],
        out_specs=FAST,
        scratch_shapes=[
            pltpu.VMEM((8, 256, WIDTH), BF16),
            pltpu.VMEM((512, WIDTH), F32),
            pltpu.VMEM((4, 8, 512, 256), BF16),
            pltpu.SemaphoreType.DMA((32,)),
        ],
        compiler_params=PARAMS,
        cost_estimate=pl.CostEstimate(
            flops=2048 * 2048 * WIDTH, bytes_accessed=2 << 20, transcendentals=0
        ),
        name="second_stage",
    )(charge_left, charge_right, got, held(masked))


def last_stage(one, two):
    return pl.pallas_call(
        last_kernel,
        grid=(4,),
        out_shape=jax.ShapeDtypeStruct((1, 512, 2 * WIDTH), F32),
        in_specs=[
            pl.BlockSpec((128, WIDTH), lambda i: (i, 0)),
            pl.BlockSpec((4, 128, WIDTH), lambda i: (0, i, 0)),
        ],
        out_specs=pl.BlockSpec((1, 128, 2 * WIDTH), lambda i: (0, i, 0)),
        name="last_stage",
    )(one, two)


def local(
    environment,
    ket_tensor,
    bra_tensor,
    charge_left,
    charge_right,
    op_in,
    op_out,
    op_bra,
    op_ket,
    op_code,
):
    left, right = charge_left.reshape(16, 128), charge_right.reshape(16, 128)
    planes = pack(ket_tensor, bra_tensor, left, right)
    gathered = lax.all_gather(planes, "chan", axis=0)

    env = lax.all_to_all(environment.reshape(16, 32, 512), "chan", 0, 0, tiled=True)
    env = env.reshape(512, 512)
    up = [(i, (i + 1) % 4) for i in range(4)]
    down = [(i, (i + 3) % 4) for i in range(4)]
    env_below = lax.ppermute(env, "ket", up)
    env_above = lax.ppermute(env, "ket", down)
    far_a = lax.ppermute(env_below[:256], "ket", up)
    far_b = lax.ppermute(env_above[256:], "ket", down)
    spread = spread_coupling(op_in, op_out, op_bra, op_ket, op_code)
    gathered, spread = lax.optimization_barrier((gathered, spread))
    pieces = (env, env_below, env_above, far_a, far_b)
    mixed, bra_quarter = zip(
        *(
            first_stage(charge_left, charge_right, pieces, gathered, left, right, spread, start)
            for start in (0, WIDTH)
        )
    )
    bra_gathered = lax.all_gather(bra_quarter[0], "ket", axis=0)
    masked = mask_bra(charge_left, charge_right, bra_gathered, left, right)
    terms = []
    for part in mixed:
        got = lax.all_to_all(part, "chan", 0, 0, tiled=True)
        terms.append(second_stage(charge_left, charge_right, got, masked))
    one = lax.psum_scatter(terms[0], "bra", scatter_dimension=0, tiled=True)
    two = lax.all_to_all(terms[1].reshape(4, 512, WIDTH), "bra", 0, 0, tiled=True)
    return last_stage(one, two)


def solution(mesh):
    placed = (
        P("chan", "bra", "ket"),
        P(None, "chan", "ket"),
        P(None, "bra", "chan"),
        P(),
        P(),
        P(),
        P(),
        P(),
        P(),
        P(),
    )
    return jax.shard_map(
        local, mesh=mesh, in_specs=placed, out_specs=P("chan", "bra", "ket"), check_vma=False
    )
```

```python
import functools

import jax
import jax.numpy as jnp
from jax import lax
from jax.experimental import pallas as pl
from jax.experimental.pallas import tpu as pltpu
from jax.sharding import PartitionSpec as P

BF16 = jnp.bfloat16
F32 = jnp.float32
PHYS = (0, 1, 1, 2)
PLANE = (0, 0, 1, 0)
WIDTH = 256


def spread_coupling(op_in, op_out, op_bra, op_ket, op_code):
    rows = jnp.arange(512, dtype=jnp.int32)
    pick_out = (rows[:, None] // 8 == (op_out * 4 + op_bra)[None, :]).astype(BF16)
    weights = op_code.astype(F32) * 0.25
    hit = (op_ket * 16 + op_in)[:, None] == rows[None, :] // 8
    pick_in = jnp.where(hit, weights[:, None], 0.0).astype(BF16)
    table = jnp.dot(pick_out, pick_in, preferred_element_type=F32)
    same = rows[:, None] % 8 == rows[None, :] % 8
    return jnp.where(same, table, 0.0).astype(BF16)


def charge_row(charges, block):
    return charges[pl.ds(block, 1), :].astype(F32)


def charge_column(charges, block):
    return jnp.transpose(jnp.broadcast_to(charge_row(charges, block), (128, 128)))


def chosen(x, diff):
    diff = diff.astype(BF16)
    return jnp.where(diff == 0, x[0], jnp.where(diff == 1, x[1], x[3]))


def pack_kernel(ket, bra, left, right, out):
    chan, y, x = lax.axis_index("chan"), lax.axis_index("ket"), lax.axis_index("bra")
    rows = charge_column(left, chan)
    for r in range(4):
        cut = slice(r * 128, (r + 1) * 128)
        diff = charge_row(right, y * 4 + r) - rows
        out[r, 0] = chosen([ket[s, :, cut] for s in range(4)], diff)
        out[r, 1] = ket[2, :, cut]
    own = pl.ds(pl.multiple_of(y * 128, 128), 128)
    diff = charge_row(right, chan) - charge_column(left, x * 4 + y)
    first = chosen([bra[t, own, :] for t in range(4)], diff)
    out[4, 0] = jnp.transpose(first.astype(F32)).astype(BF16)
    out[4, 1] = jnp.transpose(bra[2, own, :].astype(F32)).astype(BF16)


def masked_tiles(parts, rows, cols, charge):
    tiles = []
    for part, col in zip(parts, cols):
        tiles.append(jnp.where(rows + charge == col, part, jnp.zeros_like(part)))
    return jnp.concatenate(tiles, axis=1)


def begin(copies, sems):
    made = [pltpu.make_async_copy(src, dst, sems.at[n]) for n, (src, dst) in enumerate(copies)]
    for copy in made:
        copy.start()
    return made


def first_kernel(
    start, left_s, right_s, e0, e1, e2, e3a, e3b, gathered, left, right, spread,
    out, env, planes, table, column, acc, parts, results, sems, out_sems,
):
    y = lax.axis_index("ket")
    width = acc.shape[1]
    tiles = width // 128
    blocks = [lax.rem(y + n, 4) for n in (0, 3, 1, 2)]
    copies = [(gathered.at[:, pl.ds(start // 128, tiles)], planes)]
    for h in range(2):
        cut = pl.ds(h * 256, 256)
        copies += [(e.at[:, cut], env.at[2 * blocks[i] + h]) for i, e in enumerate((e0, e1, e2))]
        copies += [
            (e.at[:, cut], env.at[2 * blocks[3] + h, pl.ds(n * 256, 256)])
            for n, e in enumerate((e3a, e3b))
        ]
    copies.append((spread, table))
    copies = begin(copies, sems)
    for c in range(16):
        column[c * 128 : (c + 1) * 128, :] = charge_column(left, c).astype(BF16)
    at = y * 4 + start // 128
    cols = [charge_row(right, at + r).astype(BF16) for r in range(tiles)]
    least, most = right_s[y * 512 + start], right_s[y * 512 + start + width - 1]
    for copy in copies[:-1]:
        copy.wait()
    for s in range(4):
        acc[...] = jnp.zeros_like(acc)
        low = sum((left_s[256 * i + 255] + PHYS[s] < least).astype(jnp.int32) for i in range(8))
        high = sum((left_s[256 * i] + PHYS[s] <= most).astype(jnp.int32) for i in range(8))

        def step(i, carry):
            pair = []
            for r in range(2):
                rows = column[pl.ds(pl.multiple_of(i * 256 + r * 128, 128), 128), :]
                values = [planes[2 * i + r, q, PLANE[s]] for q in range(tiles)]
                pair.append(masked_tiles(values, rows, cols, PHYS[s]))
            block = jnp.concatenate(pair, axis=0)
            acc[...] += jnp.dot(env[i], block, preferred_element_type=F32)
            return carry

        lax.fori_loop(low, high, step, 0)
        product = acc[...].reshape(16, 4, 8, width)
        for g in range(4):
            parts[g, s * 128 : (s + 1) * 128, :] = product[:, g].reshape(128, width).astype(BF16)
    copies[-1].wait()
    sent = []
    for h in range(2):
        pair = [
            jnp.dot(table[...], parts[g], preferred_element_type=F32).reshape(16, 4, 8, width)
            for g in (2 * h, 2 * h + 1)
        ]
        results[h] = jnp.stack(pair, axis=2).reshape(16, 64, width).astype(BF16)
        copy = pltpu.make_async_copy(results.at[h], out.at[:, pl.ds(h * 64, 64)], out_sems.at[h])
        copy.start()
        sent.append(copy)
    for copy in sent:
        copy.wait()


def cut_kernel(gathered, out, held, sems, out_sems):
    parts = [pl.ds(n * 4, 4) for n in range(4)]
    loads = begin([(gathered.at[p, 4], held.at[p]) for p in parts], sems)
    sent = []
    for n, load in enumerate(loads):
        load.wait()
        copy = pltpu.make_async_copy(held.at[parts[n]], out.at[parts[n]], out_sems.at[n])
        copy.start()
        sent.append(copy)
    for copy in sent:
        copy.wait()


def active(left_s, right_s, x, g, t, h):
    least, most = right_s[g * 512], right_s[g * 512 + 511]
    first = left_s[x * 512 + h * 256] + PHYS[t]
    last = left_s[x * 512 + h * 256 + 255] + PHYS[t]
    return (first <= most) & (last >= least)


def each_active(left_s, right_s, x, act):
    for g in range(4):
        for t in range(4):
            for h in range(2):

                @pl.when(active(left_s, right_s, x, g, t, h))
                def _():
                    act(g, t * 2 + h)


def tile_copy(source, target, sems, g, n):
    return pltpu.make_async_copy(source.at[g, n], target.at[g, n], sems.at[g * 8 + n])


def mask_kernel(
    left_s, right_s, gathered, left, right, out, planes, tiles, column, sems, out_sems
):
    x = lax.axis_index("bra")
    loads = begin([(gathered.at[:, pl.ds(g * 4, 4)], planes.at[g]) for g in range(4)], sems)
    for c in range(16):
        column[c * 128 : (c + 1) * 128, :] = charge_column(right, c).astype(BF16)
    cols = [charge_row(left, x * 4 + r).astype(BF16) for r in range(4)]
    for g in range(4):
        loads[g].wait()
        for t in range(4):
            for h in range(2):

                @pl.when(active(left_s, right_s, x, g, t, h))
                def _():
                    for r in range(4):
                        rows = column[g * 512 + r * 128 : g * 512 + (r + 1) * 128, :]
                        values = [planes[g, 2 * h + q, r, PLANE[t]] for q in range(2)]
                        tile = masked_tiles(values, rows, cols[2 * h : 2 * h + 2], -PHYS[t])
                        tiles[g, t * 2 + h, r * 128 : (r + 1) * 128, :] = tile
                    tile_copy(tiles, out, out_sems, g, t * 2 + h).start()

    each_active(
        left_s, right_s, x, lambda g, n: tile_copy(tiles, out, out_sems, g, n).wait()
    )


def second_kernel(left_s, right_s, got, masked, out, mixed, acc, tiles, sems):
    x = lax.axis_index("bra")
    each_active(
        left_s, right_s, x, lambda g, n: tile_copy(masked, tiles, sems, g, n).start()
    )
    for j in range(16):
        for h in range(2):
            for t in range(4):
                at = (j % 8) * 32 + h * 16
                mixed[t * 2 + j // 8, at : at + 16, :] = got[j, h * 64 + t * 16 : h * 64 + (t + 1) * 16, :]
    for g in range(4):
        acc[...] = jnp.zeros_like(acc)
        for t in range(4):
            for h in range(2):

                @pl.when(active(left_s, right_s, x, g, t, h))
                def _():
                    n = t * 2 + h
                    tile_copy(masked, tiles, sems, g, n).wait()
                    acc[...] += jnp.dot(tiles[g, n], mixed[n], preferred_element_type=F32)

        out[g * 512 : (g + 1) * 512, :] = acc[...].astype(BF16)


SCALARS = pl.BlockSpec(memory_space=pltpu.SMEM)
FAST = pl.BlockSpec(memory_space=pltpu.VMEM)
PLACE = pl.BlockSpec(memory_space=pl.ANY)
PARAMS = pltpu.CompilerParams(vmem_limit_bytes=24 << 20)


def held(x):
    return pltpu.with_memory_space_constraint(x, pltpu.HBM)


def pack(ket_tensor, bra_tensor, left, right):
    return pl.pallas_call(
        pack_kernel,
        out_shape=jax.ShapeDtypeStruct((5, 2, 128, 128), BF16),
        in_specs=[FAST] * 4,
        out_specs=FAST,
        name="pack",
    )(ket_tensor, bra_tensor, left, right)


def first_stage(charge_left, charge_right, pieces, gathered, left, right, spread, start):
    return pl.pallas_call(
        functools.partial(first_kernel, start),
        out_shape=jax.ShapeDtypeStruct((16, 128, WIDTH), BF16),
        in_specs=[SCALARS, SCALARS] + [PLACE] * (len(pieces) + 1) + [FAST, FAST, PLACE],
        out_specs=PLACE,
        scratch_shapes=[
            pltpu.VMEM((8, 512, 256), BF16),
            pltpu.VMEM((16, WIDTH // 128, 2, 128, 128), BF16),
            pltpu.VMEM((512, 512), BF16),
            pltpu.VMEM((2048, 128), BF16),
            pltpu.VMEM((512, WIDTH), F32),
            pltpu.VMEM((4, 512, WIDTH), BF16),
            pltpu.VMEM((2, 16, 64, WIDTH), BF16),
            pltpu.SemaphoreType.DMA((12,)),
            pltpu.SemaphoreType.DMA((2,)),
        ],
        cost_estimate=pl.CostEstimate(
            flops=512 * 2048 * 4 * WIDTH, bytes_accessed=8 << 20, transcendentals=0
        ),
        name="first_stage",
    )(charge_left, charge_right, *pieces, gathered, left, right, spread)


def cut_bra(gathered):
    return pl.pallas_call(
        cut_kernel,
        out_shape=jax.ShapeDtypeStruct((16, 2, 128, 128), BF16),
        in_specs=[PLACE],
        out_specs=PLACE,
        scratch_shapes=[
            pltpu.VMEM((16, 2, 128, 128), BF16),
            pltpu.SemaphoreType.DMA((4,)),
            pltpu.SemaphoreType.DMA((4,)),
        ],
        name="cut_bra",
    )(gathered)


def mask_bra(charge_left, charge_right, gathered, left, right):
    return pl.pallas_call(
        mask_kernel,
        out_shape=pltpu.HBM((4, 8, 512, 256), BF16),
        in_specs=[SCALARS, SCALARS, PLACE, FAST, FAST],
        out_specs=PLACE,
        scratch_shapes=[
            pltpu.VMEM((4, 4, 4, 2, 128, 128), BF16),
            pltpu.VMEM((4, 8, 512, 256), BF16),
            pltpu.VMEM((2048, 128), BF16),
            pltpu.SemaphoreType.DMA((4,)),
            pltpu.SemaphoreType.DMA((32,)),
        ],
        name="mask_bra",
    )(charge_left, charge_right, held(gathered), left, right)


def second_stage(charge_left, charge_right, got, masked):
    return pl.pallas_call(
        second_kernel,
        out_shape=jax.ShapeDtypeStruct((2048, WIDTH), BF16),
        in_specs=[SCALARS, SCALARS, FAST, PLACE],
        out_specs=FAST,
        scratch_shapes=[
            pltpu.VMEM((8, 256, WIDTH), BF16),
            pltpu.VMEM((512, WIDTH), F32),
            pltpu.VMEM((4, 8, 512, 256), BF16),
            pltpu.SemaphoreType.DMA((32,)),
        ],
        compiler_params=PARAMS,
        cost_estimate=pl.CostEstimate(
            flops=2048 * 2048 * WIDTH, bytes_accessed=2 << 20, transcendentals=0
        ),
        name="second_stage",
    )(charge_left, charge_right, got, held(masked))


def local(
    environment,
    ket_tensor,
    bra_tensor,
    charge_left,
    charge_right,
    op_in,
    op_out,
    op_bra,
    op_ket,
    op_code,
):
    left, right = charge_left.reshape(16, 128), charge_right.reshape(16, 128)
    planes = pack(ket_tensor, bra_tensor, left, right)
    gathered = lax.all_gather(planes, "chan", axis=0)

    env = lax.all_to_all(environment.reshape(16, 32, 512), "chan", 0, 0, tiled=True)
    env = env.reshape(512, 512)
    up = [(i, (i + 1) % 4) for i in range(4)]
    down = [(i, (i + 3) % 4) for i in range(4)]
    env_below = lax.ppermute(env, "ket", up)
    env_above = lax.ppermute(env, "ket", down)
    far_a = lax.ppermute(env_below[:256], "ket", up)
    far_b = lax.ppermute(env_above[256:], "ket", down)
    spread = spread_coupling(op_in, op_out, op_bra, op_ket, op_code)
    pieces = (env, env_below, env_above, far_a, far_b)
    gathered, spread, pieces = lax.optimization_barrier((gathered, spread, pieces))
    bra_gathered = lax.all_gather(cut_bra(gathered), "ket", axis=0)
    masked = mask_bra(charge_left, charge_right, bra_gathered, left, right)
    terms = []
    for start in (0, WIDTH):
        mixed = first_stage(charge_left, charge_right, pieces, gathered, left, right, spread, start)
        got = lax.all_to_all(mixed, "chan", 0, 0, tiled=True)
        terms.append(second_stage(charge_left, charge_right, got, masked))
    one = lax.psum_scatter(terms[0], "bra", scatter_dimension=0, tiled=True).astype(F32)
    two = lax.all_to_all(terms[1].reshape(4, 512, WIDTH), "bra", 0, 0, tiled=True)
    two = jnp.sum(two.astype(F32), axis=0)
    return jnp.concatenate([one, two], axis=1)[None]


def solution(mesh):
    placed = (
        P("chan", "bra", "ket"),
        P(None, "chan", "ket"),
        P(None, "bra", "chan"),
        P(),
        P(),
        P(),
        P(),
        P(),
        P(),
        P(),
    )
    return jax.shard_map(
        local, mesh=mesh, in_specs=placed, out_specs=P("chan", "bra", "ket"), check_vma=False
    )
```

```python
import functools

import jax
import jax.numpy as jnp
from jax import lax
from jax.experimental import pallas as pl
from jax.experimental.pallas import tpu as pltpu
from jax.sharding import PartitionSpec as P

BF16 = jnp.bfloat16
F32 = jnp.float32
PHYS = (0, 1, 1, 2)
PLANE = (0, 0, 1, 0)
WIDTH = 256


def spread_coupling(op_in, op_out, op_bra, op_ket, op_code):
    rows = jnp.arange(512, dtype=jnp.int32)
    pick_out = (rows[:, None] // 8 == (op_out * 4 + op_bra)[None, :]).astype(BF16)
    weights = op_code.astype(F32) * 0.25
    hit = (op_ket * 16 + op_in)[:, None] == rows[None, :] // 8
    pick_in = jnp.where(hit, weights[:, None], 0.0).astype(BF16)
    table = jnp.dot(pick_out, pick_in, preferred_element_type=F32)
    same = rows[:, None] % 8 == rows[None, :] % 8
    return jnp.where(same, table, 0.0).astype(BF16)


def charge_row(charges, block):
    return charges[pl.ds(block, 1), :].astype(F32)


def charge_column(charges, block):
    return jnp.transpose(jnp.broadcast_to(charge_row(charges, block), (128, 128)))


def chosen(x, diff):
    diff = diff.astype(BF16)
    return jnp.where(diff == 0, x[0], jnp.where(diff == 1, x[1], x[3]))


def pack_kernel(ket, bra, left, right, out):
    chan, y, x = lax.axis_index("chan"), lax.axis_index("ket"), lax.axis_index("bra")
    rows = charge_column(left, chan)
    for r in range(4):
        cut = slice(r * 128, (r + 1) * 128)
        diff = charge_row(right, y * 4 + r) - rows
        out[r, 0] = chosen([ket[s, :, cut] for s in range(4)], diff)
        out[r, 1] = ket[2, :, cut]
    own = pl.ds(pl.multiple_of(y * 128, 128), 128)
    diff = charge_row(right, chan) - charge_column(left, x * 4 + y)
    first = chosen([bra[t, own, :] for t in range(4)], diff)
    out[4, 0] = jnp.transpose(first.astype(F32)).astype(BF16)
    out[4, 1] = jnp.transpose(bra[2, own, :].astype(F32)).astype(BF16)


def masked_tiles(parts, rows, cols, charge):
    tiles = []
    for part, col in zip(parts, cols):
        tiles.append(jnp.where(rows + charge == col, part, jnp.zeros_like(part)))
    return jnp.concatenate(tiles, axis=1)


def begin(copies, sems):
    made = [pltpu.make_async_copy(src, dst, sems.at[n]) for n, (src, dst) in enumerate(copies)]
    for copy in made:
        copy.start()
    return made


def first_kernel(
    start, left_s, right_s, e0, e1, e2, e3a, e3b, gathered, left, right, spread,
    out, env, planes, table, column, acc, parts, results, sems, out_sems,
):
    y = lax.axis_index("ket")
    width = acc.shape[1]
    tiles = width // 128
    blocks = [lax.rem(y + n, 4) for n in (0, 3, 1, 2)]
    copies = [(gathered.at[:, pl.ds(start // 128, tiles)], planes)]
    for h in range(2):
        cut = pl.ds(h * 256, 256)
        copies += [(e.at[:, cut], env.at[2 * blocks[i] + h]) for i, e in enumerate((e0, e1, e2))]
        copies += [
            (e.at[:, cut], env.at[2 * blocks[3] + h, pl.ds(n * 256, 256)])
            for n, e in enumerate((e3a, e3b))
        ]
    copies.append((spread, table))
    copies = begin(copies, sems)
    for c in range(16):
        column[c * 128 : (c + 1) * 128, :] = charge_column(left, c).astype(BF16)
    at = y * 4 + start // 128
    cols = [charge_row(right, at + r).astype(BF16) for r in range(tiles)]
    least, most = right_s[y * 512 + start], right_s[y * 512 + start + width - 1]
    for copy in copies[:-1]:
        copy.wait()
    for s in range(4):
        acc[...] = jnp.zeros_like(acc)
        low = sum((left_s[256 * i + 255] + PHYS[s] < least).astype(jnp.int32) for i in range(8))
        high = sum((left_s[256 * i] + PHYS[s] <= most).astype(jnp.int32) for i in range(8))

        count = (high - low + 1) // 2
        low = low - jnp.where(2 * count > high - low, jnp.minimum(low, 1), 0)

        def step(n, carry):
            i = low + 2 * n
            total = None
            for k in (i, i + 1):
                pair = []
                for r in range(2):
                    rows = column[pl.ds(pl.multiple_of(k * 256 + r * 128, 128), 128), :]
                    values = [planes[2 * k + r, q, PLANE[s]] for q in range(tiles)]
                    pair.append(masked_tiles(values, rows, cols, PHYS[s]))
                block = jnp.concatenate(pair, axis=0)
                product = jnp.dot(env[k], block, preferred_element_type=F32)
                total = product if total is None else total + product
            acc[...] += total
            return carry

        lax.fori_loop(0, count, step, 0)
        product = acc[...].reshape(16, 4, 8, width)
        for g in range(4):
            parts[g, s * 128 : (s + 1) * 128, :] = product[:, g].reshape(128, width).astype(BF16)
    copies[-1].wait()
    sent = []
    for h in range(2):
        pair = [
            jnp.dot(table[...], parts[g], preferred_element_type=F32).reshape(16, 4, 8, width)
            for g in (2 * h, 2 * h + 1)
        ]
        results[h] = jnp.stack(pair, axis=2).reshape(16, 64, width).astype(BF16)
        copy = pltpu.make_async_copy(results.at[h], out.at[:, pl.ds(h * 64, 64)], out_sems.at[h])
        copy.start()
        sent.append(copy)
    for copy in sent:
        copy.wait()


def cut_kernel(gathered, out, held, sems, out_sems):
    parts = [pl.ds(n * 4, 4) for n in range(4)]
    loads = begin([(gathered.at[p, 4], held.at[p]) for p in parts], sems)
    sent = []
    for n, load in enumerate(loads):
        load.wait()
        copy = pltpu.make_async_copy(held.at[parts[n]], out.at[parts[n]], out_sems.at[n])
        copy.start()
        sent.append(copy)
    for copy in sent:
        copy.wait()


def active(left_s, right_s, x, g, t, h):
    least, most = right_s[g * 512], right_s[g * 512 + 511]
    first = left_s[x * 512 + h * 256] + PHYS[t]
    last = left_s[x * 512 + h * 256 + 255] + PHYS[t]
    return (first <= most) & (last >= least)


def each_active(left_s, right_s, x, act):
    for g in range(4):
        for t in range(4):
            for h in range(2):

                @pl.when(active(left_s, right_s, x, g, t, h))
                def _():
                    act(g, t * 2 + h)


def tile_copy(source, target, sems, g, n):
    return pltpu.make_async_copy(source.at[g, n], target.at[g, n], sems.at[g * 8 + n])


def mask_kernel(
    left_s, right_s, gathered, left, right, out, planes, tiles, column, sems, out_sems
):
    x = lax.axis_index("bra")
    loads = begin([(gathered.at[:, pl.ds(g * 4, 4)], planes.at[g]) for g in range(4)], sems)
    for c in range(16):
        column[c * 128 : (c + 1) * 128, :] = charge_column(right, c).astype(BF16)
    cols = [charge_row(left, x * 4 + r).astype(BF16) for r in range(4)]
    for g in range(4):
        loads[g].wait()
        for t in range(4):
            for h in range(2):

                @pl.when(active(left_s, right_s, x, g, t, h))
                def _():
                    for r in range(4):
                        rows = column[g * 512 + r * 128 : g * 512 + (r + 1) * 128, :]
                        values = [planes[g, 2 * h + q, r, PLANE[t]] for q in range(2)]
                        tile = masked_tiles(values, rows, cols[2 * h : 2 * h + 2], -PHYS[t])
                        tiles[g, t * 2 + h, r * 128 : (r + 1) * 128, :] = tile
                    tile_copy(tiles, out, out_sems, g, t * 2 + h).start()

    each_active(
        left_s, right_s, x, lambda g, n: tile_copy(tiles, out, out_sems, g, n).wait()
    )


def second_kernel(left_s, right_s, got, masked, out, mixed, acc, tiles, sems):
    x = lax.axis_index("bra")
    each_active(
        left_s, right_s, x, lambda g, n: tile_copy(masked, tiles, sems, g, n).start()
    )
    for j in range(16):
        for h in range(2):
            for t in range(4):
                at = (j % 8) * 32 + h * 16
                mixed[t * 2 + j // 8, at : at + 16, :] = got[j, h * 64 + t * 16 : h * 64 + (t + 1) * 16, :]
    for g in range(4):
        acc[...] = jnp.zeros_like(acc)
        for t in range(4):
            for h in range(2):

                @pl.when(active(left_s, right_s, x, g, t, h))
                def _():
                    n = t * 2 + h
                    tile_copy(masked, tiles, sems, g, n).wait()
                    acc[...] += jnp.dot(tiles[g, n], mixed[n], preferred_element_type=F32)

        out[g * 512 : (g + 1) * 512, :] = acc[...].astype(BF16)


SCALARS = pl.BlockSpec(memory_space=pltpu.SMEM)
FAST = pl.BlockSpec(memory_space=pltpu.VMEM)
PLACE = pl.BlockSpec(memory_space=pl.ANY)
PARAMS = pltpu.CompilerParams(vmem_limit_bytes=24 << 20)


def held(x):
    return pltpu.with_memory_space_constraint(x, pltpu.HBM)


def pack(ket_tensor, bra_tensor, left, right):
    return pl.pallas_call(
        pack_kernel,
        out_shape=jax.ShapeDtypeStruct((5, 2, 128, 128), BF16),
        in_specs=[FAST] * 4,
        out_specs=FAST,
        name="pack",
    )(ket_tensor, bra_tensor, left, right)


def first_stage(charge_left, charge_right, pieces, gathered, left, right, spread, start):
    return pl.pallas_call(
        functools.partial(first_kernel, start),
        out_shape=jax.ShapeDtypeStruct((16, 128, WIDTH), BF16),
        in_specs=[SCALARS, SCALARS] + [PLACE] * (len(pieces) + 1) + [FAST, FAST, PLACE],
        out_specs=PLACE,
        scratch_shapes=[
            pltpu.VMEM((8, 512, 256), BF16),
            pltpu.VMEM((16, WIDTH // 128, 2, 128, 128), BF16),
            pltpu.VMEM((512, 512), BF16),
            pltpu.VMEM((2048, 128), BF16),
            pltpu.VMEM((512, WIDTH), F32),
            pltpu.VMEM((4, 512, WIDTH), BF16),
            pltpu.VMEM((2, 16, 64, WIDTH), BF16),
            pltpu.SemaphoreType.DMA((12,)),
            pltpu.SemaphoreType.DMA((2,)),
        ],
        cost_estimate=pl.CostEstimate(
            flops=512 * 2048 * 4 * WIDTH, bytes_accessed=8 << 20, transcendentals=0
        ),
        name="first_stage",
    )(charge_left, charge_right, *pieces, gathered, left, right, spread)


def cut_bra(gathered):
    return pl.pallas_call(
        cut_kernel,
        out_shape=jax.ShapeDtypeStruct((16, 2, 128, 128), BF16),
        in_specs=[PLACE],
        out_specs=PLACE,
        scratch_shapes=[
            pltpu.VMEM((16, 2, 128, 128), BF16),
            pltpu.SemaphoreType.DMA((4,)),
            pltpu.SemaphoreType.DMA((4,)),
        ],
        name="cut_bra",
    )(gathered)


def mask_bra(charge_left, charge_right, gathered, left, right):
    return pl.pallas_call(
        mask_kernel,
        out_shape=pltpu.HBM((4, 8, 512, 256), BF16),
        in_specs=[SCALARS, SCALARS, PLACE, FAST, FAST],
        out_specs=PLACE,
        scratch_shapes=[
            pltpu.VMEM((4, 4, 4, 2, 128, 128), BF16),
            pltpu.VMEM((4, 8, 512, 256), BF16),
            pltpu.VMEM((2048, 128), BF16),
            pltpu.SemaphoreType.DMA((4,)),
            pltpu.SemaphoreType.DMA((32,)),
        ],
        name="mask_bra",
    )(charge_left, charge_right, held(gathered), left, right)


def second_stage(charge_left, charge_right, got, masked):
    return pl.pallas_call(
        second_kernel,
        out_shape=jax.ShapeDtypeStruct((2048, WIDTH), BF16),
        in_specs=[SCALARS, SCALARS, FAST, PLACE],
        out_specs=FAST,
        scratch_shapes=[
            pltpu.VMEM((8, 256, WIDTH), BF16),
            pltpu.VMEM((512, WIDTH), F32),
            pltpu.VMEM((4, 8, 512, 256), BF16),
            pltpu.SemaphoreType.DMA((32,)),
        ],
        compiler_params=PARAMS,
        cost_estimate=pl.CostEstimate(
            flops=2048 * 2048 * WIDTH, bytes_accessed=2 << 20, transcendentals=0
        ),
        name="second_stage",
    )(charge_left, charge_right, got, held(masked))


def local(
    environment,
    ket_tensor,
    bra_tensor,
    charge_left,
    charge_right,
    op_in,
    op_out,
    op_bra,
    op_ket,
    op_code,
):
    left, right = charge_left.reshape(16, 128), charge_right.reshape(16, 128)
    planes = pack(ket_tensor, bra_tensor, left, right)
    gathered = lax.all_gather(planes, "chan", axis=0)

    env = lax.all_to_all(environment.reshape(16, 32, 512), "chan", 0, 0, tiled=True)
    env = env.reshape(512, 512)
    up = [(i, (i + 1) % 4) for i in range(4)]
    down = [(i, (i + 3) % 4) for i in range(4)]
    env_below = lax.ppermute(env, "ket", up)
    env_above = lax.ppermute(env, "ket", down)
    far_a = lax.ppermute(env_below[:256], "ket", up)
    far_b = lax.ppermute(env_above[256:], "ket", down)
    spread = spread_coupling(op_in, op_out, op_bra, op_ket, op_code)
    pieces = (env, env_below, env_above, far_a, far_b)
    gathered, spread, pieces = lax.optimization_barrier((gathered, spread, pieces))
    bra_gathered = lax.all_gather(cut_bra(gathered), "ket", axis=0)
    masked = mask_bra(charge_left, charge_right, bra_gathered, left, right)
    terms = []
    for start in (0, WIDTH):
        mixed = first_stage(charge_left, charge_right, pieces, gathered, left, right, spread, start)
        got = lax.all_to_all(mixed, "chan", 0, 0, tiled=True)
        terms.append(second_stage(charge_left, charge_right, got, masked))
    one = lax.psum_scatter(terms[0], "bra", scatter_dimension=0, tiled=True).astype(F32)
    two = lax.all_to_all(terms[1].reshape(4, 512, WIDTH), "bra", 0, 0, tiled=True)
    two = jnp.sum(two.astype(F32), axis=0)
    return jnp.concatenate([one, two], axis=1)[None]


def solution(mesh):
    placed = (
        P("chan", "bra", "ket"),
        P(None, "chan", "ket"),
        P(None, "bra", "chan"),
        P(),
        P(),
        P(),
        P(),
        P(),
        P(),
        P(),
    )
    return jax.shard_map(
        local, mesh=mesh, in_specs=placed, out_specs=P("chan", "bra", "ket"), check_vma=False
    )
```

```python
import functools

import jax
import jax.numpy as jnp
from jax import lax
from jax.experimental import pallas as pl
from jax.experimental.pallas import tpu as pltpu
from jax.sharding import PartitionSpec as P

BF16 = jnp.bfloat16
F32 = jnp.float32
PHYS = (0, 1, 1, 2)
PLANE = (0, 0, 1, 0)
WIDTH = 256


def spread_coupling(op_in, op_out, op_bra, op_ket, op_code):
    rows = jnp.arange(512, dtype=jnp.int32)
    pick_out = (rows[:, None] // 8 == (op_out * 4 + op_bra)[None, :]).astype(BF16)
    weights = op_code.astype(F32) * 0.25
    hit = (op_ket * 16 + op_in)[:, None] == rows[None, :] // 8
    pick_in = jnp.where(hit, weights[:, None], 0.0).astype(BF16)
    table = jnp.dot(pick_out, pick_in, preferred_element_type=F32)
    same = rows[:, None] % 8 == rows[None, :] % 8
    return jnp.where(same, table, 0.0).astype(BF16)


def charge_row(charges, block):
    return charges[pl.ds(block, 1), :].astype(F32)


def charge_column(charges, block):
    return jnp.transpose(jnp.broadcast_to(charge_row(charges, block), (128, 128)))


def chosen(x, diff):
    diff = diff.astype(BF16)
    return jnp.where(diff == 0, x[0], jnp.where(diff == 1, x[1], x[3]))


def pack_kernel(ket, bra, left, right, out):
    chan, y, x = lax.axis_index("chan"), lax.axis_index("ket"), lax.axis_index("bra")
    rows = charge_column(left, chan)
    for r in range(4):
        cut = slice(r * 128, (r + 1) * 128)
        diff = charge_row(right, y * 4 + r) - rows
        out[r, 0] = chosen([ket[s, :, cut] for s in range(4)], diff)
        out[r, 1] = ket[2, :, cut]
    own = pl.ds(pl.multiple_of(y * 128, 128), 128)
    diff = charge_row(right, chan) - charge_column(left, x * 4 + y)
    first = chosen([bra[t, own, :] for t in range(4)], diff)
    out[4, 0] = jnp.transpose(first.astype(F32)).astype(BF16)
    out[4, 1] = jnp.transpose(bra[2, own, :].astype(F32)).astype(BF16)


def masked_tiles(parts, rows, cols, charge):
    tiles = []
    for part, col in zip(parts, cols):
        tiles.append(jnp.where(rows + charge == col, part, jnp.zeros_like(part)))
    return jnp.concatenate(tiles, axis=1)


def begin(copies, sems):
    made = [pltpu.make_async_copy(src, dst, sems.at[n]) for n, (src, dst) in enumerate(copies)]
    for copy in made:
        copy.start()
    return made


def first_kernel(
    start, left_s, right_s, e0, e1, e2, e3, e4, e5, e6, e7, gathered, left, right, spread,
    out, env, planes, table, column, acc, parts, results, sems, out_sems,
):
    y = lax.axis_index("ket")
    width = acc.shape[1]
    tiles = width // 128
    blocks = [lax.rem(y + n, 4) for n in (0, 3, 1, 2)]
    copies = [(gathered.at[:, pl.ds(start // 128, tiles)], planes)]
    for h in range(2):
        cut = pl.ds(h * 256, 256)
        copies += [
            (e.at[:, cut], env.at[2 * blocks[n // 2] + h, pl.ds(n % 2 * 256, 256)])
            for n, e in enumerate((e0, e1, e2, e3, e4, e5, e6, e7))
        ]
    copies.append((spread, table))
    copies = begin(copies, sems)
    for c in range(16):
        column[c * 128 : (c + 1) * 128, :] = charge_column(left, c).astype(BF16)
    at = y * 4 + start // 128
    cols = [charge_row(right, at + r).astype(BF16) for r in range(tiles)]
    least, most = right_s[y * 512 + start], right_s[y * 512 + start + width - 1]
    for copy in copies[:-1]:
        copy.wait()
    for s in range(4):
        acc[...] = jnp.zeros_like(acc)
        low = sum((left_s[256 * i + 255] + PHYS[s] < least).astype(jnp.int32) for i in range(8))
        high = sum((left_s[256 * i] + PHYS[s] <= most).astype(jnp.int32) for i in range(8))

        count = (high - low + 1) // 2
        low = low - jnp.where(2 * count > high - low, jnp.minimum(low, 1), 0)

        def step(n, carry):
            i = low + 2 * n
            total = None
            for k in (i, i + 1):
                pair = []
                for r in range(2):
                    rows = column[pl.ds(pl.multiple_of(k * 256 + r * 128, 128), 128), :]
                    values = [planes[2 * k + r, q, PLANE[s]] for q in range(tiles)]
                    pair.append(masked_tiles(values, rows, cols, PHYS[s]))
                block = jnp.concatenate(pair, axis=0)
                product = jnp.dot(env[k], block, preferred_element_type=F32)
                total = product if total is None else total + product
            acc[...] += total
            return carry

        lax.fori_loop(0, count, step, 0)
        product = acc[...].reshape(16, 4, 8, width)
        for g in range(4):
            parts[g, s * 128 : (s + 1) * 128, :] = product[:, g].reshape(128, width).astype(BF16)
    copies[-1].wait()
    sent = []
    for h in range(2):
        pair = [
            jnp.dot(table[...], parts[g], preferred_element_type=F32).reshape(16, 4, 8, width)
            for g in (2 * h, 2 * h + 1)
        ]
        results[h] = jnp.stack(pair, axis=2).reshape(16, 64, width).astype(BF16)
        copy = pltpu.make_async_copy(results.at[h], out.at[:, pl.ds(h * 64, 64)], out_sems.at[h])
        copy.start()
        sent.append(copy)
    for copy in sent:
        copy.wait()


def cut_kernel(gathered, out, held, sems, out_sems):
    parts = [pl.ds(n * 4, 4) for n in range(4)]
    loads = begin([(gathered.at[p, 4], held.at[p]) for p in parts], sems)
    sent = []
    for n, load in enumerate(loads):
        load.wait()
        copy = pltpu.make_async_copy(held.at[parts[n]], out.at[parts[n]], out_sems.at[n])
        copy.start()
        sent.append(copy)
    for copy in sent:
        copy.wait()


def active(left_s, right_s, x, g, t, h):
    least, most = right_s[g * 512], right_s[g * 512 + 511]
    first = left_s[x * 512 + h * 256] + PHYS[t]
    last = left_s[x * 512 + h * 256 + 255] + PHYS[t]
    return (first <= most) & (last >= least)


def each_active(left_s, right_s, x, act):
    for g in range(4):
        for t in range(4):
            for h in range(2):

                @pl.when(active(left_s, right_s, x, g, t, h))
                def _():
                    act(g, t * 2 + h)


def tile_copy(source, target, sems, g, n):
    return pltpu.make_async_copy(source.at[g, n], target.at[g, n], sems.at[g * 8 + n])


def mask_kernel(
    left_s, right_s, gathered, left, right, out, planes, tiles, column, sems, out_sems
):
    x = lax.axis_index("bra")
    loads = begin([(gathered.at[:, pl.ds(g * 4, 4)], planes.at[g]) for g in range(4)], sems)
    for c in range(16):
        column[c * 128 : (c + 1) * 128, :] = charge_column(right, c).astype(BF16)
    cols = [charge_row(left, x * 4 + r).astype(BF16) for r in range(4)]
    for g in range(4):
        loads[g].wait()
        for t in range(4):
            for h in range(2):

                @pl.when(active(left_s, right_s, x, g, t, h))
                def _():
                    for r in range(4):
                        rows = column[g * 512 + r * 128 : g * 512 + (r + 1) * 128, :]
                        values = [planes[g, 2 * h + q, r, PLANE[t]] for q in range(2)]
                        tile = masked_tiles(values, rows, cols[2 * h : 2 * h + 2], -PHYS[t])
                        tiles[g, t * 2 + h, r * 128 : (r + 1) * 128, :] = tile
                    tile_copy(tiles, out, out_sems, g, t * 2 + h).start()

    each_active(
        left_s, right_s, x, lambda g, n: tile_copy(tiles, out, out_sems, g, n).wait()
    )


def second_kernel(left_s, right_s, got, masked, out, mixed, acc, tiles, sems):
    x = lax.axis_index("bra")
    each_active(
        left_s, right_s, x, lambda g, n: tile_copy(masked, tiles, sems, g, n).start()
    )
    for j in range(16):
        for h in range(2):
            for t in range(4):
                at = (j % 8) * 32 + h * 16
                mixed[t * 2 + j // 8, at : at + 16, :] = got[j, h * 64 + t * 16 : h * 64 + (t + 1) * 16, :]
    for g in range(4):
        acc[...] = jnp.zeros_like(acc)
        for t in range(4):
            for h in range(2):

                @pl.when(active(left_s, right_s, x, g, t, h))
                def _():
                    n = t * 2 + h
                    tile_copy(masked, tiles, sems, g, n).wait()
                    acc[...] += jnp.dot(tiles[g, n], mixed[n], preferred_element_type=F32)

        out[g * 512 : (g + 1) * 512, :] = acc[...].astype(BF16)


SCALARS = pl.BlockSpec(memory_space=pltpu.SMEM)
FAST = pl.BlockSpec(memory_space=pltpu.VMEM)
PLACE = pl.BlockSpec(memory_space=pl.ANY)
PARAMS = pltpu.CompilerParams(vmem_limit_bytes=24 << 20)


def held(x):
    return pltpu.with_memory_space_constraint(x, pltpu.HBM)


def pack(ket_tensor, bra_tensor, left, right):
    return pl.pallas_call(
        pack_kernel,
        out_shape=jax.ShapeDtypeStruct((5, 2, 128, 128), BF16),
        in_specs=[FAST] * 4,
        out_specs=FAST,
        name="pack",
    )(ket_tensor, bra_tensor, left, right)


def first_stage(charge_left, charge_right, pieces, gathered, left, right, spread, start):
    return pl.pallas_call(
        functools.partial(first_kernel, start),
        out_shape=jax.ShapeDtypeStruct((16, 128, WIDTH), BF16),
        in_specs=[SCALARS, SCALARS] + [PLACE] * (len(pieces) + 1) + [FAST, FAST, PLACE],
        out_specs=PLACE,
        scratch_shapes=[
            pltpu.VMEM((8, 512, 256), BF16),
            pltpu.VMEM((16, WIDTH // 128, 2, 128, 128), BF16),
            pltpu.VMEM((512, 512), BF16),
            pltpu.VMEM((2048, 128), BF16),
            pltpu.VMEM((512, WIDTH), F32),
            pltpu.VMEM((4, 512, WIDTH), BF16),
            pltpu.VMEM((2, 16, 64, WIDTH), BF16),
            pltpu.SemaphoreType.DMA((18,)),
            pltpu.SemaphoreType.DMA((2,)),
        ],
        cost_estimate=pl.CostEstimate(
            flops=512 * 2048 * 4 * WIDTH, bytes_accessed=8 << 20, transcendentals=0
        ),
        name="first_stage",
    )(charge_left, charge_right, *pieces, gathered, left, right, spread)


def cut_bra(gathered):
    return pl.pallas_call(
        cut_kernel,
        out_shape=jax.ShapeDtypeStruct((16, 2, 128, 128), BF16),
        in_specs=[PLACE],
        out_specs=PLACE,
        scratch_shapes=[
            pltpu.VMEM((16, 2, 128, 128), BF16),
            pltpu.SemaphoreType.DMA((4,)),
            pltpu.SemaphoreType.DMA((4,)),
        ],
        name="cut_bra",
    )(gathered)


def mask_bra(charge_left, charge_right, gathered, left, right):
    return pl.pallas_call(
        mask_kernel,
        out_shape=pltpu.HBM((4, 8, 512, 256), BF16),
        in_specs=[SCALARS, SCALARS, PLACE, FAST, FAST],
        out_specs=PLACE,
        scratch_shapes=[
            pltpu.VMEM((4, 4, 4, 2, 128, 128), BF16),
            pltpu.VMEM((4, 8, 512, 256), BF16),
            pltpu.VMEM((2048, 128), BF16),
            pltpu.SemaphoreType.DMA((4,)),
            pltpu.SemaphoreType.DMA((32,)),
        ],
        name="mask_bra",
    )(charge_left, charge_right, held(gathered), left, right)


def second_stage(charge_left, charge_right, got, masked):
    return pl.pallas_call(
        second_kernel,
        out_shape=jax.ShapeDtypeStruct((2048, WIDTH), BF16),
        in_specs=[SCALARS, SCALARS, FAST, PLACE],
        out_specs=FAST,
        scratch_shapes=[
            pltpu.VMEM((8, 256, WIDTH), BF16),
            pltpu.VMEM((512, WIDTH), F32),
            pltpu.VMEM((4, 8, 512, 256), BF16),
            pltpu.SemaphoreType.DMA((32,)),
        ],
        compiler_params=PARAMS,
        cost_estimate=pl.CostEstimate(
            flops=2048 * 2048 * WIDTH, bytes_accessed=2 << 20, transcendentals=0
        ),
        name="second_stage",
    )(charge_left, charge_right, got, held(masked))


def local(
    environment,
    ket_tensor,
    bra_tensor,
    charge_left,
    charge_right,
    op_in,
    op_out,
    op_bra,
    op_ket,
    op_code,
):
    left, right = charge_left.reshape(16, 128), charge_right.reshape(16, 128)
    planes = pack(ket_tensor, bra_tensor, left, right)
    gathered = lax.all_gather(planes, "chan", axis=0)

    env = lax.all_to_all(environment.reshape(16, 32, 512), "chan", 0, 0, tiled=True)
    env = env.reshape(512, 512)
    up = [(i, (i + 1) % 4) for i in range(4)]
    down = [(i, (i + 3) % 4) for i in range(4)]
    low, high = env[:256], env[256:]
    below_low = lax.ppermute(low, "ket", up)
    above_high = lax.ppermute(high, "ket", down)
    below_high = lax.ppermute(high, "ket", up)
    above_low = lax.ppermute(low, "ket", down)
    far_low = lax.ppermute(below_low, "ket", up)
    far_high = lax.ppermute(above_high, "ket", down)
    spread = spread_coupling(op_in, op_out, op_bra, op_ket, op_code)
    pieces = (low, high, below_low, below_high, above_low, above_high, far_low, far_high)
    gathered, spread, pieces = lax.optimization_barrier((gathered, spread, pieces))
    bra_gathered = lax.all_gather(cut_bra(gathered), "ket", axis=0)
    masked = mask_bra(charge_left, charge_right, bra_gathered, left, right)
    terms = []
    for start in (0, WIDTH):
        mixed = first_stage(charge_left, charge_right, pieces, gathered, left, right, spread, start)
        got = lax.all_to_all(mixed, "chan", 0, 0, tiled=True)
        terms.append(second_stage(charge_left, charge_right, got, masked))
    one = lax.psum_scatter(terms[0], "bra", scatter_dimension=0, tiled=True).astype(F32)
    two = lax.all_to_all(terms[1].reshape(4, 512, WIDTH), "bra", 0, 0, tiled=True)
    two = jnp.sum(two.astype(F32), axis=0)
    return jnp.concatenate([one, two], axis=1)[None]


def solution(mesh):
    placed = (
        P("chan", "bra", "ket"),
        P(None, "chan", "ket"),
        P(None, "bra", "chan"),
        P(),
        P(),
        P(),
        P(),
        P(),
        P(),
        P(),
    )
    return jax.shard_map(
        local, mesh=mesh, in_specs=placed, out_specs=P("chan", "bra", "ket"), check_vma=False
    )
```
